128 devices in a mesh: row: 8 (over z_lo, y), col: 16 (over z_hi, x, core).
Axes of the slice: x: 4, y: 4, z: 4 (z_hi: 2, z_lo: 2; z = z_hi * 2 + z_lo), core: 2. Of those that a mesh axis runs over, the one named last changes fastest.
Arguments:
- init_temp: float32 [4, 2048, 8192], P(None, 'row', 'col'), may hold values from -6 to 6
- power: float32 [8192, 64, 64], P(('row', 'col')), may hold values from 0 to 3
- die_owner: int32 [8192, 1], P(('row', 'col')), may hold values from 0 to 127; in each aligned block of 64 rows (0 to 63, 64 to 127, ...) at most 2 rows name the same one
- die_tile: int32 [8192], P(('row', 'col')), may hold values from 0 to 31
- classes: int32 [4, 2048, 8192], P(None, 'row', 'col'), may hold values from 0 to 7
- cond_table: float32 [4, 8], replicated, may hold values from 0.2 to 1.5
- target: float32 [2048, 8192], P('row', 'col'), may hold values from -6 to 6
Outputs:
- final_temp: float32 [4, 2048, 8192], P(None, 'row', 'col')
- init_grad: float32 [4, 2048, 8192], P(None, 'row', 'col')
- die_grad: float32 [8192, 64, 64], P(('row', 'col'))
The draws below stay inside these ranges and needn't reach their ends.
Inputs may be any that keep to these rules, and one draw needn't show every extreme that they name: `die_owner`: among the dies of one device (aligned blocks of 64 dies), at most 2 have the same owner.
All inputs are finite; a program needn't handle non-finite values.
Results may differ from the reference program's by a relative error of at most 0.000088.
Values sent between devices are 32-bit elements; how exact they have to be, the bound alone decides.
A program may use at most 128 MiB of HBM per device.

```python
import math
import jax
import jax.numpy as jnp
import numpy as np

LAYERS = 4
TILE = 64
CLASSES = 8
STEPS = 6
CAP = 2
DIE_DEV = 64
CR = 256
CC = 512
NR = 2048
NC = 8192
DIES = 8192
TPD = 32
N_ROW = 8
N_COL = 16
DEVICES = 128


def plant(values, stream_key, smallest, top_value):
    spot = [jax.random.randint(jax.random.fold_in(stream_key, axis), (), 0, length) for axis, length in enumerate(values.shape)]
    widest = values.shape.index(max(values.shape))
    next_to = spot[:widest] + [(spot[widest] + 1) % values.shape[widest]] + spot[widest + 1:]
    return values.at[tuple(spot)].set(smallest).at[tuple(next_to)].set(top_value)


def level_of(stream_key, shape, split, least, largest):
    def one(dim, blocks):
        heights = jax.random.uniform(jax.random.fold_in(jax.random.fold_in(stream_key, 6), dim), (blocks,), jnp.float32, least / len(split), largest / len(split))
        return jnp.repeat(jnp.exp(heights), shape[dim] // blocks).reshape((-1,) + (1,) * (len(shape) - dim - 1))

    level = one(*split[0])
    for cut in split[1:]:
        level = level * one(*cut)
    return level


def routed_block(own_key, own, number, rows, count, top, limit, skew):
    sequence = jax.random.permutation(own_key, count)
    packed, usual = portions_of(count, rows * top, limit, skew, True), portions_of(count, rows * top, limit, skew, False)
    places = jnp.arange(count)

    def named(sizes, rotation):
        used = int((sizes > 0).sum())
        fixed = max(1, used // 4)
        moved = fixed + (places - fixed + rotation * (used - fixed)) % max(1, count - fixed)
        return jnp.zeros((count,), jnp.int32).at[sequence[jnp.where(places < fixed, places, moved)]].set(jnp.asarray(sizes, jnp.int32))

    sizes = jnp.where(number % 4 == 0, named(packed, number // 4), named(usual, number - number // 4 - 1))
    mixed = jax.random.permutation(jax.random.fold_in(own, 3), count)
    source_of, receiver = mixed[0:count // 2 * 2:2], mixed[1:count // 2 * 2:2]
    room = jnp.minimum(sizes[source_of] - 1, limit - sizes[receiver]) // 2
    room = jnp.where((source_of == sequence[0]) | (receiver == sequence[0]) | (sizes[receiver] == 0), 0, jnp.maximum(room, 0))
    moved = jax.random.randint(jax.random.fold_in(own, 4), (count // 2,), 0, 1 << 20) % (room + 1)
    sizes = sizes.at[source_of].add(-moved).at[receiver].add(moved)
    labels = jnp.searchsorted(jnp.cumsum(sizes), jnp.arange(rows * top), side="right").astype(jnp.int32)
    listing = labels.reshape(top, rows).T
    listing = listing[jax.random.permutation(jax.random.fold_in(own, 1), rows)]
    rotation = jax.random.randint(jax.random.fold_in(own, 2), (rows, 1), 0, top)
    return jnp.take_along_axis(listing, (jnp.arange(top)[None, :] + rotation) % top, axis=1)


def portions_of(amount, total, most, lean, full):
    loads = [(1 << 20) // math.isqrt(grade ** lean) + 1 for grade in range(1, amount + 1)]
    largest = most if full else min(most, max(-(-total // amount), total * loads[0] // sum(loads)))
    least = 1 if total - largest >= amount - 1 else 0
    counts, rest = [largest] + [least] * (amount - 1), total - largest - least * (amount - 1)
    while rest > 0:
        movable = [i for i in range(1, amount) if counts[i] < largest] or [i for i in range(1, amount) if counts[i] < most]
        pool, left = sum([loads[i] for i in movable]), rest
        for i in movable:
            addition = min(most - counts[i], max(1, left * loads[i] // pool), rest)
            counts[i] = counts[i] + addition
            rest = rest - addition
    return np.array(counts)


def centred(stream_key, dims, deviation, limit, cuts=(), held_as=jnp.bfloat16):
    factor_of = level_of(stream_key, dims, cuts, -0.22, 0.18) if cuts else 1.0
    values = jax.random.normal(stream_key, dims, jnp.float32) * deviation * factor_of
    return jnp.minimum(jnp.maximum(values, -limit), limit).astype(held_as)


def setup_inputs(seed: int = 0) -> dict:
    streams_of = jax.random.split(jax.random.key(seed), 8)
    init_temp = centred(streams_of[0], (LAYERS, NR, NC), 1.0, 6.0, ((1, 8), (2, 16)), jnp.float32)
    power = jnp.clip(3.0 * jax.random.uniform(streams_of[1], (DIES, TILE, TILE), jnp.float32) ** level_of(streams_of[1], (DIES, TILE, TILE), ((0, 128),), -0.2, 0.2), 0.0, 3.0)
    die_owner_keys = jax.random.split(jax.random.fold_in(streams_of[2], 1), DIES // DIE_DEV)
    die_owner_turns = jax.random.permutation(jax.random.fold_in(streams_of[2], 3), DIES // DIE_DEV)
    die_owner = jax.vmap(lambda own, number: routed_block(jax.random.fold_in(streams_of[2], 2), own, number, DIE_DEV, DEVICES, 1, CAP, 2))(die_owner_keys, die_owner_turns).reshape((DIES, 1))
    die_tile = plant(jax.random.randint(streams_of[3], (DIES,), 0, TPD), jax.random.fold_in(streams_of[3], 1), 0, TPD - 1).astype(jnp.int32)
    classes = plant(jax.random.randint(streams_of[4], (LAYERS, NR, NC), 0, CLASSES), jax.random.fold_in(streams_of[4], 1), 0, CLASSES - 1).astype(jnp.int32)
    cond_table = jnp.clip(jax.random.uniform(streams_of[5], (LAYERS, CLASSES), jnp.float32, 0.2, 1.5), 0.2, 1.5)
    target = centred(streams_of[6], (NR, NC), 1.0, 6.0, ((0, 8), (1, 16)), jnp.float32)
    return dict(init_temp=init_temp, power=power, die_owner=die_owner, die_tile=die_tile, classes=classes, cond_table=cond_table, target=target)


RATE = 0.1
AMBIENT_LOSS = 0.3

def conduct_root(classes, cond_table):
    conduct = jnp.zeros(classes.shape, cond_table.dtype)
    for label in range(CLASSES):
        conduct = conduct + jnp.where(classes == label, cond_table[:, label][:, None, None], 0.0)
    return jnp.sqrt(conduct)

def advance(field, root_cond, source):
    middle = field[:, 1:-1, 1:-1]
    roots = root_cond[:, 1:-1, 1:-1]
    inflow = roots * root_cond[:, :-2, 1:-1] * (field[:, :-2, 1:-1] - middle)
    inflow = inflow + roots * root_cond[:, 2:, 1:-1] * (field[:, 2:, 1:-1] - middle)
    inflow = inflow + roots * root_cond[:, 1:-1, :-2] * (field[:, 1:-1, :-2] - middle)
    inflow = inflow + roots * root_cond[:, 1:-1, 2:] * (field[:, 1:-1, 2:] - middle)
    vertical = roots[1:] * roots[:-1] * (middle[1:] - middle[:-1])
    zero_layer = jnp.zeros_like(middle[:1])
    inflow = inflow + jnp.concatenate([vertical, zero_layer], 0) - jnp.concatenate([zero_layer, vertical], 0)
    inflow = inflow - AMBIENT_LOSS * jnp.concatenate([jnp.zeros_like(middle[:-1]), middle[-1:]], 0)
    if source is not None:
        inflow = inflow + jnp.concatenate([source[None], jnp.zeros_like(middle[1:])], 0)
    return middle + RATE * inflow

def pad_rim(field):
    return jnp.pad(field, ((0, 0), (1, 1), (1, 1)))

def reference(init_temp, power, die_owner, die_tile, classes, cond_table, target):
    tile_rows = CR // TILE
    tile_cols = CC // TILE
    grid_rows = N_ROW * tile_rows
    grid_cols = N_COL * tile_cols
    height = CR * N_ROW
    breadth = CC * N_COL
    owners = die_owner[:, 0]
    global_tile = (owners // N_COL * tile_rows + die_tile // tile_cols) * grid_cols + owners % N_COL * tile_cols + die_tile % tile_cols
    global_tile = global_tile.astype(jnp.int32)
    power_flat = power.reshape(power.shape[0], TILE * TILE)
    source_tiles = jax.ops.segment_sum(power_flat, global_tile, num_segments=grid_rows * grid_cols)
    source = source_tiles.reshape(grid_rows, grid_cols, TILE, TILE).transpose(0, 2, 1, 3).reshape(height, breadth)
    padded_roots = pad_rim(conduct_root(classes, cond_table))
    heat_field = init_temp
    for step_index in range(STEPS):
        heat_field = advance(pad_rim(heat_field), padded_roots, source)
    adjoint = jnp.concatenate([(heat_field[0] - target)[None], jnp.zeros_like(heat_field[1:])], 0)
    grad_sum = jnp.zeros_like(target)
    for step_index in range(STEPS):
        grad_sum = grad_sum + adjoint[0]
        adjoint = advance(pad_rim(adjoint), padded_roots, None)
    grad_tiles = grad_sum.reshape(grid_rows, TILE, grid_cols, TILE).transpose(0, 2, 1, 3).reshape(grid_rows * grid_cols, TILE * TILE)
    die_grad = (RATE * grad_tiles[global_tile]).reshape(power.shape)
    return (heat_field, adjoint, die_grad)
```

```python
import jax
import jax.numpy as jnp
from jax import lax
from jax.sharding import PartitionSpec as P

TILE = 64
CLASSES = 8
STEPS = 6
CAP = 2


RATE = 0.1
AMBIENT_LOSS = 0.3


def extended(cells, sides, width):
    for axis, dim in sides:
        count = lax.axis_size(axis)
        ends = count - 1
        head = lax.slice_in_dim(cells, 0, width, axis=dim)
        tail = lax.slice_in_dim(cells, cells.shape[dim] - width, cells.shape[dim], axis=dim)
        cells = jnp.concatenate(
            [
                lax.ppermute(tail, axis, [(i, (i + 1) % count) for i in range(ends)]),
                cells,
                lax.ppermute(head, axis, [((i + 1) % count, i) for i in range(ends)]),
            ],
            axis=dim,
        )
    return cells


def conduct_root(classes, cond_table):
    conduct = jnp.zeros(classes.shape, cond_table.dtype)
    for label in range(CLASSES):
        conduct = conduct + jnp.where(classes == label, cond_table[:, label][:, None, None], 0.0)
    return jnp.sqrt(conduct)


def advance(field, root_cond, source):
    middle = field[:, 1:-1, 1:-1]
    roots = root_cond[:, 1:-1, 1:-1]
    inflow = roots * root_cond[:, :-2, 1:-1] * (field[:, :-2, 1:-1] - middle)
    inflow = inflow + roots * root_cond[:, 2:, 1:-1] * (field[:, 2:, 1:-1] - middle)
    inflow = inflow + roots * root_cond[:, 1:-1, :-2] * (field[:, 1:-1, :-2] - middle)
    inflow = inflow + roots * root_cond[:, 1:-1, 2:] * (field[:, 1:-1, 2:] - middle)
    vertical = roots[1:] * roots[:-1] * (middle[1:] - middle[:-1])
    zero_layer = jnp.zeros_like(middle[:1])
    inflow = (
        inflow
        + jnp.concatenate([vertical, zero_layer], 0)
        - jnp.concatenate([zero_layer, vertical], 0)
    )
    inflow = inflow - AMBIENT_LOSS * jnp.concatenate([jnp.zeros_like(middle[:-1]), middle[-1:]], 0)
    if source is not None:
        inflow = inflow + jnp.concatenate([source[None], jnp.zeros_like(middle[1:])], 0)
    return middle + RATE * inflow


def step_rim(field):
    return extended(field, (("row", 1), ("col", 2)), 1)


def send_dies(outbound, tile_ids, row_count, col_count):
    received, recv_tiles = (
        lax.all_to_all(
            outbound.reshape(row_count * col_count, CAP, -1),
            ("row", "col"),
            split_axis=0,
            concat_axis=0,
            tiled=True,
        ),
        lax.all_to_all(
            tile_ids.reshape(row_count * col_count, CAP),
            ("row", "col"),
            split_axis=0,
            concat_axis=0,
            tiled=True,
        ),
    )
    return (
        received.reshape(row_count * col_count * CAP, -1),
        recv_tiles.reshape(row_count * col_count * CAP),
    )


def return_grads(backward, row_count, col_count):
    returned = lax.all_to_all(
        backward.reshape(row_count * col_count, CAP, -1),
        ("row", "col"),
        split_axis=0,
        concat_axis=0,
        tiled=True,
    )
    return returned.reshape(row_count * col_count * CAP, -1)


def on_device(init_temp, power, die_owner, die_tile, classes, cond_table, target):
    row_count = lax.axis_size("row")
    col_count = lax.axis_size("col")
    devices_all = row_count * col_count
    layers, height, breadth = init_temp.shape
    tile_rows = height // TILE
    tile_cols = breadth // TILE
    die_count = power.shape[0]
    highest = lax.Precision.HIGHEST
    power_flat = power.reshape(die_count, TILE * TILE)
    owners = die_owner[:, 0]
    ordinal = jnp.arange(die_count, dtype=jnp.int32)
    same_owner = (owners[:, None] == owners[None, :]) & (ordinal[:, None] < ordinal[None, :])
    ranking = jnp.sum(same_owner.astype(jnp.int32), axis=0)
    slot_index = owners * CAP + ranking
    all_slots = jnp.arange(devices_all * CAP, dtype=jnp.int32)
    matched = all_slots[:, None] == slot_index[None, :]
    send_hot = matched.astype(jnp.float32)
    outbound = jnp.dot(send_hot, power_flat, precision=highest)
    tile_ids = jnp.sum(jnp.where(matched, die_tile[None, :] + 1, 0), axis=1) - 1
    received, recv_tiles = send_dies(outbound, tile_ids, row_count, col_count)
    tile_range = jnp.arange(tile_rows * tile_cols, dtype=jnp.int32)
    recv_hot = (tile_range[:, None] == recv_tiles[None, :]).astype(jnp.float32)
    source_tiles = jnp.dot(recv_hot, received, precision=highest)
    source = (
        source_tiles.reshape(tile_rows, tile_cols, TILE, TILE)
        .transpose(0, 2, 1, 3)
        .reshape(height, breadth)
    )
    root_cond = conduct_root(classes, cond_table)
    sides = (("row", 1), ("col", 2))
    reach = STEPS
    padded_roots = extended(root_cond, sides, reach)
    padded_source = extended(source[None], sides, reach)[0]
    heat_field = extended(init_temp, sides, reach)
    for step_index in range(STEPS):
        edge = step_index
        inner = edge + 1
        heat_field = advance(
            heat_field,
            padded_roots[:, edge : edge + heat_field.shape[1], edge : edge + heat_field.shape[2]],
            padded_source[inner : inner + heat_field.shape[1] - 2, inner : inner + heat_field.shape[2] - 2],
        )
    start = extended((heat_field[0] - target)[None], sides, reach)
    adjoint = jnp.concatenate([start, jnp.zeros((layers - 1,) + start.shape[1:], start.dtype)], 0)
    grad_sum = jnp.zeros_like(target)
    for step_index in range(STEPS):
        edge = reach - step_index
        grad_sum = grad_sum + adjoint[0, edge : edge + height, edge : edge + breadth]
        adjoint = advance(
            adjoint,
            padded_roots[:, step_index : step_index + adjoint.shape[1], step_index : step_index + adjoint.shape[2]],
            None,
        )
    grad_tiles = (
        grad_sum.reshape(tile_rows, TILE, tile_cols, TILE)
        .transpose(0, 2, 1, 3)
        .reshape(tile_rows * tile_cols, TILE * TILE)
    )
    backward = jnp.dot(recv_hot.T, grad_tiles, precision=highest)
    returned = return_grads(backward, row_count, col_count)
    die_grad = (RATE * jnp.dot(send_hot.T, returned, precision=highest)).reshape(
        die_count, TILE, TILE
    )
    return (heat_field, adjoint, die_grad)


def solution(mesh):
    in_specs = (
        P(None, "row", "col"),
        P(("row", "col"), None, None),
        P(("row", "col"), None),
        P(("row", "col")),
        P(None, "row", "col"),
        P(),
        P("row", "col"),
    )
    out_specs = (P(None, "row", "col"), P(None, "row", "col"), P(("row", "col"), None, None))
    return jax.shard_map(
        on_device, mesh=mesh, in_specs=in_specs, out_specs=out_specs, check_vma=False
    )
```

```python
import jax
import jax.numpy as jnp
from jax import lax
from jax.experimental import pallas as pl
from jax.experimental.pallas import tpu as pltpu
from jax.sharding import PartitionSpec as P

TILE = 64
CLASSES = 8
STEPS = 6
CAP = 2


RATE = 0.1
AMBIENT_LOSS = 0.3


def extended(cells, sides, width):
    for axis, dim in sides:
        count = lax.axis_size(axis)
        ends = count - 1
        head = lax.slice_in_dim(cells, 0, width, axis=dim)
        tail = lax.slice_in_dim(cells, cells.shape[dim] - width, cells.shape[dim], axis=dim)
        cells = jnp.concatenate(
            [
                lax.ppermute(tail, axis, [(i, (i + 1) % count) for i in range(ends)]),
                cells,
                lax.ppermute(head, axis, [((i + 1) % count, i) for i in range(ends)]),
            ],
            axis=dim,
        )
    return cells


def conduct_root(classes, cond_table):
    conduct = jnp.zeros(classes.shape, cond_table.dtype)
    for label in range(CLASSES):
        conduct = conduct + jnp.where(classes == label, cond_table[:, label][:, None, None], 0.0)
    return jnp.sqrt(conduct)


def advance(field, root_cond, source):
    middle = field[:, 1:-1, 1:-1]
    roots = root_cond[:, 1:-1, 1:-1]
    inflow = roots * root_cond[:, :-2, 1:-1] * (field[:, :-2, 1:-1] - middle)
    inflow = inflow + roots * root_cond[:, 2:, 1:-1] * (field[:, 2:, 1:-1] - middle)
    inflow = inflow + roots * root_cond[:, 1:-1, :-2] * (field[:, 1:-1, :-2] - middle)
    inflow = inflow + roots * root_cond[:, 1:-1, 2:] * (field[:, 1:-1, 2:] - middle)
    vertical = roots[1:] * roots[:-1] * (middle[1:] - middle[:-1])
    zero_layer = jnp.zeros_like(middle[:1])
    inflow = (
        inflow
        + jnp.concatenate([vertical, zero_layer], 0)
        - jnp.concatenate([zero_layer, vertical], 0)
    )
    inflow = inflow - AMBIENT_LOSS * jnp.concatenate([jnp.zeros_like(middle[:-1]), middle[-1:]], 0)
    if source is not None:
        inflow = inflow + jnp.concatenate([source[None], jnp.zeros_like(middle[1:])], 0)
    return middle + RATE * inflow


HALO = 8
SLACK = 8
CHUNK = 16
LANE = 128


def framed(cells):
    depth, height, breadth = cells.shape
    cols = lax.axis_size("col")
    rows = lax.axis_size("row")
    left = lax.ppermute(cells[:, :, breadth - HALO :], "col", [(i, i + 1) for i in range(cols - 1)])
    right = lax.ppermute(cells[:, :, :HALO], "col", [(i + 1, i) for i in range(cols - 1)])
    gap = jnp.zeros((depth, height, LANE - 2 * HALO), cells.dtype)
    band = jnp.concatenate([cells, right, gap, left], axis=2)
    top = lax.ppermute(band[:, height - HALO :], "row", [(i, i + 1) for i in range(rows - 1)])
    bottom = lax.ppermute(band[:, :HALO], "row", [(i + 1, i) for i in range(rows - 1)])
    pad = jnp.zeros((depth, SLACK, band.shape[2]), cells.dtype)
    return jnp.concatenate([pad, top, band, bottom, pad], axis=1)


def chunk_loop(count, body):
    lax.fori_loop(0, count, lambda c, carry: (body(c), carry)[1], 0)


def conductances(r_ref, cu, cd, cl, cr, cv):
    layers, frame_rows, frame_cols = r_ref.shape
    count = (frame_rows - 2 * SLACK) // CHUNK

    def body(c):
        lead = pl.multiple_of(c * CHUNK, 8)
        rows = pl.ds(pl.multiple_of(lead + SLACK, 8), CHUNK)
        for l in range(layers):
            win = r_ref[l, pl.ds(lead, CHUNK + 2 * SLACK), :]
            r = win[SLACK : SLACK + CHUNK]
            cu[l, rows, :] = r * pltpu.roll(win, 1, 0)[SLACK : SLACK + CHUNK]
            cd[l, rows, :] = r * pltpu.roll(win, CHUNK + 2 * SLACK - 1, 0)[SLACK : SLACK + CHUNK]
            cl[l, rows, :] = r * pltpu.roll(r, 1, 1)
            cr[l, rows, :] = r * pltpu.roll(r, frame_cols - 1, 1)
            if l + 1 < layers:
                cv[l, rows, :] = r_ref[l + 1, rows, :] * r

    chunk_loop(count, body)


def explicit_step(src, dst, cu, cd, cl, cr, cv, s_ref):
    layers, frame_rows, frame_cols = dst.shape
    count = (frame_rows - 2 * SLACK) // CHUNK

    def body(c):
        lead = pl.multiple_of(c * CHUNK, 8)
        rows = pl.ds(pl.multiple_of(lead + SLACK, 8), CHUNK)
        for l in range(layers):
            win = src[l, pl.ds(lead, CHUNK + 2 * SLACK), :]
            f = win[SLACK : SLACK + CHUNK]
            up = pltpu.roll(win, 1, 0)[SLACK : SLACK + CHUNK]
            down = pltpu.roll(win, CHUNK + 2 * SLACK - 1, 0)[SLACK : SLACK + CHUNK]
            left = pltpu.roll(f, 1, 1)
            right = pltpu.roll(f, frame_cols - 1, 1)
            inflow = cu[l, rows, :] * (up - f)
            inflow = inflow + cd[l, rows, :] * (down - f)
            inflow = inflow + cl[l, rows, :] * (left - f)
            inflow = inflow + cr[l, rows, :] * (right - f)
            if l + 1 < layers:
                inflow = inflow + cv[l, rows, :] * (src[l + 1, rows, :] - f)
            if l > 0:
                inflow = inflow - cv[l - 1, rows, :] * (f - src[l - 1, rows, :])
            if l == layers - 1:
                inflow = inflow - AMBIENT_LOSS * f
            if l == 0 and s_ref is not None:
                inflow = inflow + s_ref[rows, :]
            dst[l, rows, :] = f + RATE * inflow

    chunk_loop(count, body)


def clear_slack(buf):
    layers, frame_rows, frame_cols = buf.shape
    zero = jnp.zeros((layers, SLACK, frame_cols), buf.dtype)
    buf[:, 0:SLACK, :] = zero
    buf[:, frame_rows - SLACK : frame_rows, :] = zero


def copy_center(src_view, dst_ref, height, breadth):
    def body(c):
        rows = pl.ds(pl.multiple_of(c * CHUNK, 8), CHUNK)
        from_rows = pl.ds(pl.multiple_of(c * CHUNK + SLACK + HALO, 8), CHUNK)
        dst_ref(rows, src_view(from_rows, breadth))

    chunk_loop(height // CHUNK, body)


def forward_kernel(f_ref, r_ref, s_ref, out_ref, cu, cd, cl, cr, cv, a, b):
    layers, height, breadth = out_ref.shape
    clear_slack(a)
    clear_slack(b)
    conductances(r_ref, cu, cd, cl, cr, cv)
    src = f_ref
    for index in range(STEPS):
        dst = a if index % 2 == 0 else b
        explicit_step(src, dst, cu, cd, cl, cr, cv, s_ref)
        src = dst

    def put(rows, value):
        out_ref[:, rows, :] = value

    copy_center(lambda rows, width: src[:, rows, 0:width], put, height, breadth)


def adjoint_kernel(a0_ref, r_ref, grad_ref, gsum_ref, cu, cd, cl, cr, cv, a, b):
    layers, height, breadth = grad_ref.shape
    a[...] = jnp.zeros(a.shape, a.dtype)
    clear_slack(b)
    a[0] = a0_ref[...]
    conductances(r_ref, cu, cd, cl, cr, cv)
    src = a
    for index in range(STEPS):
        view = src

        def put_sum(rows, value, first=(index == 0)):
            if first:
                gsum_ref[rows, :] = value
            else:
                gsum_ref[rows, :] = gsum_ref[rows, :] + value

        copy_center(lambda rows, width, v=view: v[0, rows, 0:width], put_sum, height, breadth)
        dst = b if index % 2 == 0 else a
        explicit_step(src, dst, cu, cd, cl, cr, cv, None)
        src = dst

    def put(rows, value):
        grad_ref[:, rows, :] = value

    copy_center(lambda rows, width: src[:, rows, 0:width], put, height, breadth)


def stencil_scratch(layers, frame_rows, frame_cols):
    whole = pltpu.VMEM((layers, frame_rows, frame_cols), jnp.float32)
    return [whole] * 4 + [pltpu.VMEM((layers - 1, frame_rows, frame_cols), jnp.float32), whole, whole]


def vmem_specs(count):
    return [pl.BlockSpec(memory_space=pltpu.VMEM) for _ in range(count)]


def run_forward(f_frame, r_frame, s_frame, height, breadth):
    layers, frame_rows, frame_cols = f_frame.shape
    return pl.pallas_call(
        forward_kernel,
        out_shape=jax.ShapeDtypeStruct((layers, height, breadth), jnp.float32),
        in_specs=vmem_specs(3),
        out_specs=vmem_specs(1)[0],
        scratch_shapes=stencil_scratch(layers, frame_rows, frame_cols),
        compiler_params=pltpu.CompilerParams(vmem_limit_bytes=56 * 1024 * 1024),
    )(f_frame, r_frame, s_frame)


def run_adjoint(a0_frame, r_frame, height, breadth):
    layers, frame_rows, frame_cols = r_frame.shape
    return pl.pallas_call(
        adjoint_kernel,
        out_shape=(
            jax.ShapeDtypeStruct((layers, height, breadth), jnp.float32),
            jax.ShapeDtypeStruct((height, breadth), jnp.float32),
        ),
        in_specs=vmem_specs(2),
        out_specs=tuple(vmem_specs(2)),
        scratch_shapes=stencil_scratch(layers, frame_rows, frame_cols),
        compiler_params=pltpu.CompilerParams(vmem_limit_bytes=56 * 1024 * 1024),
    )(a0_frame, r_frame)


def send_dies(outbound, tile_ids, row_count, col_count):
    received, recv_tiles = (
        lax.all_to_all(
            outbound.reshape(row_count * col_count, CAP, -1),
            ("row", "col"),
            split_axis=0,
            concat_axis=0,
            tiled=True,
        ),
        lax.all_to_all(
            tile_ids.reshape(row_count * col_count, CAP),
            ("row", "col"),
            split_axis=0,
            concat_axis=0,
            tiled=True,
        ),
    )
    return (
        received.reshape(row_count * col_count * CAP, -1),
        recv_tiles.reshape(row_count * col_count * CAP),
    )


def return_grads(backward, row_count, col_count):
    returned = lax.all_to_all(
        backward.reshape(row_count * col_count, CAP, -1),
        ("row", "col"),
        split_axis=0,
        concat_axis=0,
        tiled=True,
    )
    return returned.reshape(row_count * col_count * CAP, -1)


def on_device(init_temp, power, die_owner, die_tile, classes, cond_table, target):
    row_count = lax.axis_size("row")
    col_count = lax.axis_size("col")
    devices_all = row_count * col_count
    layers, height, breadth = init_temp.shape
    tile_rows = height // TILE
    tile_cols = breadth // TILE
    die_count = power.shape[0]
    highest = lax.Precision.HIGHEST
    power_flat = power.reshape(die_count, TILE * TILE)
    owners = die_owner[:, 0]
    ordinal = jnp.arange(die_count, dtype=jnp.int32)
    same_owner = (owners[:, None] == owners[None, :]) & (ordinal[:, None] < ordinal[None, :])
    ranking = jnp.sum(same_owner.astype(jnp.int32), axis=0)
    slot_index = owners * CAP + ranking
    all_slots = jnp.arange(devices_all * CAP, dtype=jnp.int32)
    matched = all_slots[:, None] == slot_index[None, :]
    send_hot = matched.astype(jnp.float32)
    outbound = jnp.dot(send_hot, power_flat, precision=highest)
    tile_ids = jnp.sum(jnp.where(matched, die_tile[None, :] + 1, 0), axis=1) - 1
    received, recv_tiles = send_dies(outbound, tile_ids, row_count, col_count)
    tile_range = jnp.arange(tile_rows * tile_cols, dtype=jnp.int32)
    recv_hot = (tile_range[:, None] == recv_tiles[None, :]).astype(jnp.float32)
    source_tiles = jnp.dot(recv_hot, received, precision=highest)
    source = (
        source_tiles.reshape(tile_rows, tile_cols, TILE, TILE)
        .transpose(0, 2, 1, 3)
        .reshape(height, breadth)
    )
    root_cond = conduct_root(classes, cond_table)
    r_frame = framed(root_cond)
    s_frame = framed(source[None])[0]
    f_frame = framed(init_temp)
    heat_field = run_forward(f_frame, r_frame, s_frame, height, breadth)
    a0_frame = framed((heat_field[0] - target)[None])[0]
    adjoint, grad_sum = run_adjoint(a0_frame, r_frame, height, breadth)
    grad_tiles = (
        grad_sum.reshape(tile_rows, TILE, tile_cols, TILE)
        .transpose(0, 2, 1, 3)
        .reshape(tile_rows * tile_cols, TILE * TILE)
    )
    backward = jnp.dot(recv_hot.T, grad_tiles, precision=highest)
    returned = return_grads(backward, row_count, col_count)
    die_grad = (RATE * jnp.dot(send_hot.T, returned, precision=highest)).reshape(
        die_count, TILE, TILE
    )
    return (heat_field, adjoint, die_grad)


def solution(mesh):
    in_specs = (
        P(None, "row", "col"),
        P(("row", "col"), None, None),
        P(("row", "col"), None),
        P(("row", "col")),
        P(None, "row", "col"),
        P(),
        P("row", "col"),
    )
    out_specs = (P(None, "row", "col"), P(None, "row", "col"), P(("row", "col"), None, None))
    return jax.shard_map(
        on_device, mesh=mesh, in_specs=in_specs, out_specs=out_specs, check_vma=False
    )
```

```python
import jax
import jax.numpy as jnp
from jax import lax
from jax.experimental import pallas as pl
from jax.experimental.pallas import tpu as pltpu
from jax.sharding import PartitionSpec as P

TILE = 64
CLASSES = 8
STEPS = 6
CAP = 2


RATE = 0.1
AMBIENT_LOSS = 0.3


def extended(cells, sides, width):
    for axis, dim in sides:
        count = lax.axis_size(axis)
        ends = count - 1
        head = lax.slice_in_dim(cells, 0, width, axis=dim)
        tail = lax.slice_in_dim(cells, cells.shape[dim] - width, cells.shape[dim], axis=dim)
        cells = jnp.concatenate(
            [
                lax.ppermute(tail, axis, [(i, (i + 1) % count) for i in range(ends)]),
                cells,
                lax.ppermute(head, axis, [((i + 1) % count, i) for i in range(ends)]),
            ],
            axis=dim,
        )
    return cells


def conduct_root(classes, cond_table):
    conduct = jnp.zeros(classes.shape, cond_table.dtype)
    for label in range(CLASSES):
        conduct = conduct + jnp.where(classes == label, cond_table[:, label][:, None, None], 0.0)
    return jnp.sqrt(conduct)


def advance(field, root_cond, source):
    middle = field[:, 1:-1, 1:-1]
    roots = root_cond[:, 1:-1, 1:-1]
    inflow = roots * root_cond[:, :-2, 1:-1] * (field[:, :-2, 1:-1] - middle)
    inflow = inflow + roots * root_cond[:, 2:, 1:-1] * (field[:, 2:, 1:-1] - middle)
    inflow = inflow + roots * root_cond[:, 1:-1, :-2] * (field[:, 1:-1, :-2] - middle)
    inflow = inflow + roots * root_cond[:, 1:-1, 2:] * (field[:, 1:-1, 2:] - middle)
    vertical = roots[1:] * roots[:-1] * (middle[1:] - middle[:-1])
    zero_layer = jnp.zeros_like(middle[:1])
    inflow = (
        inflow
        + jnp.concatenate([vertical, zero_layer], 0)
        - jnp.concatenate([zero_layer, vertical], 0)
    )
    inflow = inflow - AMBIENT_LOSS * jnp.concatenate([jnp.zeros_like(middle[:-1]), middle[-1:]], 0)
    if source is not None:
        inflow = inflow + jnp.concatenate([source[None], jnp.zeros_like(middle[1:])], 0)
    return middle + RATE * inflow


HALO = 8
SLACK = 8
CHUNK = 16
LANE = 128


def framed(cells):
    depth, height, breadth = cells.shape
    cols = lax.axis_size("col")
    rows = lax.axis_size("row")
    left = lax.ppermute(
        jnp.swapaxes(cells[:, :, breadth - HALO :], 1, 2), "col", [(i, i + 1) for i in range(cols - 1)]
    )
    right = lax.ppermute(jnp.swapaxes(cells[:, :, :HALO], 1, 2), "col", [(i + 1, i) for i in range(cols - 1)])
    left = jnp.swapaxes(left, 1, 2)
    right = jnp.swapaxes(right, 1, 2)
    gap = jnp.zeros((depth, height, LANE - 2 * HALO), cells.dtype)
    band = jnp.concatenate([cells, right, gap, left], axis=2)
    top = lax.ppermute(band[:, height - HALO :], "row", [(i, i + 1) for i in range(rows - 1)])
    bottom = lax.ppermute(band[:, :HALO], "row", [(i + 1, i) for i in range(rows - 1)])
    pad = jnp.zeros((depth, SLACK, band.shape[2]), cells.dtype)
    return jnp.concatenate([pad, top, band, bottom, pad], axis=1)


def chunk_loop(count, body):
    lax.fori_loop(0, count, lambda c, carry: (body(c), carry)[1], 0)


def conductances(r_ref, cu, cd, cl, cr, cv):
    layers, frame_rows, frame_cols = r_ref.shape
    count = (frame_rows - 2 * SLACK) // CHUNK

    def body(c):
        lead = pl.multiple_of(c * CHUNK, 8)
        rows = pl.ds(pl.multiple_of(lead + SLACK, 8), CHUNK)
        for l in range(layers):
            win = r_ref[l, pl.ds(lead, CHUNK + 2 * SLACK), :]
            r = win[SLACK : SLACK + CHUNK]
            cu[l, rows, :] = r * pltpu.roll(win, 1, 0)[SLACK : SLACK + CHUNK]
            cd[l, rows, :] = r * pltpu.roll(win, CHUNK + 2 * SLACK - 1, 0)[SLACK : SLACK + CHUNK]
            cl[l, rows, :] = r * pltpu.roll(r, 1, 1)
            cr[l, rows, :] = r * pltpu.roll(r, frame_cols - 1, 1)
            if l + 1 < layers:
                cv[l, rows, :] = r_ref[l + 1, rows, :] * r

    chunk_loop(count, body)


def explicit_step(src, dst, cu, cd, cl, cr, cv, s_ref):
    layers, frame_rows, frame_cols = dst.shape
    count = (frame_rows - 2 * SLACK) // CHUNK

    def body(c):
        lead = pl.multiple_of(c * CHUNK, 8)
        rows = pl.ds(pl.multiple_of(lead + SLACK, 8), CHUNK)
        for l in range(layers):
            win = src[l, pl.ds(lead, CHUNK + 2 * SLACK), :]
            f = win[SLACK : SLACK + CHUNK]
            up = pltpu.roll(win, 1, 0)[SLACK : SLACK + CHUNK]
            down = pltpu.roll(win, CHUNK + 2 * SLACK - 1, 0)[SLACK : SLACK + CHUNK]
            left = pltpu.roll(f, 1, 1)
            right = pltpu.roll(f, frame_cols - 1, 1)
            inflow = cu[l, rows, :] * (up - f)
            inflow = inflow + cd[l, rows, :] * (down - f)
            inflow = inflow + cl[l, rows, :] * (left - f)
            inflow = inflow + cr[l, rows, :] * (right - f)
            if l + 1 < layers:
                inflow = inflow + cv[l, rows, :] * (src[l + 1, rows, :] - f)
            if l > 0:
                inflow = inflow - cv[l - 1, rows, :] * (f - src[l - 1, rows, :])
            if l == layers - 1:
                inflow = inflow - AMBIENT_LOSS * f
            if l == 0 and s_ref is not None:
                inflow = inflow + s_ref[rows, :]
            dst[l, rows, :] = f + RATE * inflow

    chunk_loop(count, body)


def clear_slack(buf):
    layers, frame_rows, frame_cols = buf.shape
    zero = jnp.zeros((layers, SLACK, frame_cols), buf.dtype)
    buf[:, 0:SLACK, :] = zero
    buf[:, frame_rows - SLACK : frame_rows, :] = zero


def copy_center(src_view, dst_ref, height, breadth):
    def body(c):
        rows = pl.ds(pl.multiple_of(c * CHUNK, 8), CHUNK)
        from_rows = pl.ds(pl.multiple_of(c * CHUNK + SLACK + HALO, 8), CHUNK)
        dst_ref(rows, src_view(from_rows, breadth))

    chunk_loop(height // CHUNK, body)


def forward_kernel(f_ref, r_ref, s_ref, out_ref, cu, cd, cl, cr, cv, a, b):
    layers, height, breadth = out_ref.shape
    clear_slack(a)
    clear_slack(b)
    conductances(r_ref, cu, cd, cl, cr, cv)
    src = f_ref
    for index in range(STEPS):
        dst = a if index % 2 == 0 else b
        explicit_step(src, dst, cu, cd, cl, cr, cv, s_ref)
        src = dst

    def put(rows, value):
        out_ref[:, rows, :] = value

    copy_center(lambda rows, width: src[:, rows, 0:width], put, height, breadth)


def adjoint_kernel(a0_ref, r_ref, grad_ref, gsum_ref, cu, cd, cl, cr, cv, a, b):
    layers, height, breadth = grad_ref.shape
    a[...] = jnp.zeros(a.shape, a.dtype)
    clear_slack(b)
    a[0] = a0_ref[...]
    conductances(r_ref, cu, cd, cl, cr, cv)
    src = a
    for index in range(STEPS):
        view = src

        def put_sum(rows, value, first=(index == 0)):
            if first:
                gsum_ref[rows, :] = value
            else:
                gsum_ref[rows, :] = gsum_ref[rows, :] + value

        copy_center(lambda rows, width, v=view: v[0, rows, 0:width], put_sum, height, breadth)
        dst = b if index % 2 == 0 else a
        explicit_step(src, dst, cu, cd, cl, cr, cv, None)
        src = dst

    def put(rows, value):
        grad_ref[:, rows, :] = value

    copy_center(lambda rows, width: src[:, rows, 0:width], put, height, breadth)


def stencil_scratch(layers, frame_rows, frame_cols):
    whole = pltpu.VMEM((layers, frame_rows, frame_cols), jnp.float32)
    return [whole] * 4 + [pltpu.VMEM((layers - 1, frame_rows, frame_cols), jnp.float32), whole, whole]


def vmem_specs(count):
    return [pl.BlockSpec(memory_space=pltpu.VMEM) for _ in range(count)]


def run_forward(f_frame, r_frame, s_frame, height, breadth):
    layers, frame_rows, frame_cols = f_frame.shape
    return pl.pallas_call(
        forward_kernel,
        out_shape=jax.ShapeDtypeStruct((layers, height, breadth), jnp.float32),
        in_specs=vmem_specs(3),
        out_specs=vmem_specs(1)[0],
        scratch_shapes=stencil_scratch(layers, frame_rows, frame_cols),
        compiler_params=pltpu.CompilerParams(vmem_limit_bytes=56 * 1024 * 1024),
    )(f_frame, r_frame, s_frame)


def run_adjoint(a0_frame, r_frame, height, breadth):
    layers, frame_rows, frame_cols = r_frame.shape
    return pl.pallas_call(
        adjoint_kernel,
        out_shape=(
            jax.ShapeDtypeStruct((layers, height, breadth), jnp.float32),
            jax.ShapeDtypeStruct((height, breadth), jnp.float32),
        ),
        in_specs=vmem_specs(2),
        out_specs=tuple(vmem_specs(2)),
        scratch_shapes=stencil_scratch(layers, frame_rows, frame_cols),
        compiler_params=pltpu.CompilerParams(vmem_limit_bytes=56 * 1024 * 1024),
    )(a0_frame, r_frame)


def send_dies(outbound, row_count, col_count):
    received = lax.all_to_all(
        outbound.reshape(row_count * col_count, CAP, -1),
        ("row", "col"),
        split_axis=0,
        concat_axis=0,
        tiled=True,
    )
    return received.reshape(row_count * col_count * CAP, -1)


def return_grads(backward, row_count, col_count):
    returned = lax.all_to_all(
        backward.reshape(row_count * col_count, CAP, -1),
        ("row", "col"),
        split_axis=0,
        concat_axis=0,
        tiled=True,
    )
    return returned.reshape(row_count * col_count * CAP, -1)


def on_device(init_temp, power, die_owner, die_tile, classes, cond_table, target):
    row_count = lax.axis_size("row")
    col_count = lax.axis_size("col")
    devices_all = row_count * col_count
    layers, height, breadth = init_temp.shape
    tile_rows = height // TILE
    tile_cols = breadth // TILE
    die_count = power.shape[0]
    highest = lax.Precision.HIGHEST
    power_flat = power.reshape(die_count, TILE * TILE)
    owners = die_owner[:, 0]
    ordinal = jnp.arange(die_count, dtype=jnp.int32)
    same_owner = (owners[:, None] == owners[None, :]) & (ordinal[:, None] < ordinal[None, :])
    ranking = jnp.sum(same_owner.astype(jnp.int32), axis=0)
    slot_index = owners * CAP + ranking
    all_slots = jnp.arange(devices_all * CAP, dtype=jnp.int32)
    matched = all_slots[:, None] == slot_index[None, :]
    send_hot = matched.astype(jnp.float32)
    tile_column = jnp.zeros((die_count, LANE), jnp.float32).at[:, 0].set((die_tile + 1).astype(jnp.float32))
    outbound = jnp.dot(send_hot, jnp.concatenate([power_flat, tile_column], 1), precision=highest)
    received = send_dies(outbound, row_count, col_count)
    recv_tiles = received[:, TILE * TILE].astype(jnp.int32) - 1
    received = received[:, : TILE * TILE]
    tile_range = jnp.arange(tile_rows * tile_cols, dtype=jnp.int32)
    recv_hot = (tile_range[:, None] == recv_tiles[None, :]).astype(jnp.float32)
    source_tiles = jnp.dot(recv_hot, received, precision=highest)
    source = (
        source_tiles.reshape(tile_rows, tile_cols, TILE, TILE)
        .transpose(0, 2, 1, 3)
        .reshape(height, breadth)
    )
    root_cond = conduct_root(classes, cond_table)
    r_frame = framed(root_cond)
    s_frame = framed(source[None])[0]
    f_frame = framed(init_temp)
    heat_field = run_forward(f_frame, r_frame, s_frame, height, breadth)
    a0_frame = framed((heat_field[0] - target)[None])[0]
    adjoint, grad_sum = run_adjoint(a0_frame, r_frame, height, breadth)
    grad_tiles = (
        grad_sum.reshape(tile_rows, TILE, tile_cols, TILE)
        .transpose(0, 2, 1, 3)
        .reshape(tile_rows * tile_cols, TILE * TILE)
    )
    backward = jnp.dot(recv_hot.T, grad_tiles, precision=highest)
    returned = return_grads(backward, row_count, col_count)
    die_grad = (RATE * jnp.dot(send_hot.T, returned, precision=highest)).reshape(
        die_count, TILE, TILE
    )
    return (heat_field, adjoint, die_grad)


def solution(mesh):
    in_specs = (
        P(None, "row", "col"),
        P(("row", "col"), None, None),
        P(("row", "col"), None),
        P(("row", "col")),
        P(None, "row", "col"),
        P(),
        P("row", "col"),
    )
    out_specs = (P(None, "row", "col"), P(None, "row", "col"), P(("row", "col"), None, None))
    return jax.shard_map(
        on_device, mesh=mesh, in_specs=in_specs, out_specs=out_specs, check_vma=False
    )
```

```python
import jax
import jax.numpy as jnp
from jax import lax
from jax.experimental import pallas as pl
from jax.experimental.pallas import tpu as pltpu
from jax.sharding import PartitionSpec as P

TILE = 64
CLASSES = 8
STEPS = 6
CAP = 2


RATE = 0.1
AMBIENT_LOSS = 0.3


def extended(cells, sides, width):
    for axis, dim in sides:
        count = lax.axis_size(axis)
        ends = count - 1
        head = lax.slice_in_dim(cells, 0, width, axis=dim)
        tail = lax.slice_in_dim(cells, cells.shape[dim] - width, cells.shape[dim], axis=dim)
        cells = jnp.concatenate(
            [
                lax.ppermute(tail, axis, [(i, (i + 1) % count) for i in range(ends)]),
                cells,
                lax.ppermute(head, axis, [((i + 1) % count, i) for i in range(ends)]),
            ],
            axis=dim,
        )
    return cells


def conduct_root(classes, cond_table):
    conduct = jnp.zeros(classes.shape, cond_table.dtype)
    for label in range(CLASSES):
        conduct = conduct + jnp.where(classes == label, cond_table[:, label][:, None, None], 0.0)
    return jnp.sqrt(conduct)


def advance(field, root_cond, source):
    middle = field[:, 1:-1, 1:-1]
    roots = root_cond[:, 1:-1, 1:-1]
    inflow = roots * root_cond[:, :-2, 1:-1] * (field[:, :-2, 1:-1] - middle)
    inflow = inflow + roots * root_cond[:, 2:, 1:-1] * (field[:, 2:, 1:-1] - middle)
    inflow = inflow + roots * root_cond[:, 1:-1, :-2] * (field[:, 1:-1, :-2] - middle)
    inflow = inflow + roots * root_cond[:, 1:-1, 2:] * (field[:, 1:-1, 2:] - middle)
    vertical = roots[1:] * roots[:-1] * (middle[1:] - middle[:-1])
    zero_layer = jnp.zeros_like(middle[:1])
    inflow = (
        inflow
        + jnp.concatenate([vertical, zero_layer], 0)
        - jnp.concatenate([zero_layer, vertical], 0)
    )
    inflow = inflow - AMBIENT_LOSS * jnp.concatenate([jnp.zeros_like(middle[:-1]), middle[-1:]], 0)
    if source is not None:
        inflow = inflow + jnp.concatenate([source[None], jnp.zeros_like(middle[1:])], 0)
    return middle + RATE * inflow


HALO = 8
SLACK = 8
CHUNK = 16
LANE = 128


def framed(cells):
    depth, height, breadth = cells.shape
    cols = lax.axis_size("col")
    rows = lax.axis_size("row")
    left = lax.ppermute(
        jnp.swapaxes(cells[:, :, breadth - HALO :], 1, 2), "col", [(i, i + 1) for i in range(cols - 1)]
    )
    right = lax.ppermute(jnp.swapaxes(cells[:, :, :HALO], 1, 2), "col", [(i + 1, i) for i in range(cols - 1)])
    left = jnp.swapaxes(left, 1, 2)
    right = jnp.swapaxes(right, 1, 2)
    gap = jnp.zeros((depth, height, LANE - 2 * HALO), cells.dtype)
    band = jnp.concatenate([cells, right, gap, left], axis=2)
    top = lax.ppermute(band[:, height - HALO :], "row", [(i, i + 1) for i in range(rows - 1)])
    bottom = lax.ppermute(band[:, :HALO], "row", [(i + 1, i) for i in range(rows - 1)])
    pad = jnp.zeros((depth, SLACK, band.shape[2]), cells.dtype)
    return jnp.concatenate([pad, top, band, bottom, pad], axis=1)


def chunk_loop(count, body):
    lax.fori_loop(0, count, lambda c, carry: (body(c), carry)[1], 0)


def conductances(r_ref, cu, cd, cl, cr, cv):
    layers, frame_rows, frame_cols = r_ref.shape
    count = (frame_rows - 2 * SLACK) // CHUNK

    def body(c):
        lead = pl.multiple_of(c * CHUNK, 8)
        rows = pl.ds(pl.multiple_of(lead + SLACK, 8), CHUNK)
        for l in range(layers):
            win = r_ref[l, pl.ds(lead, CHUNK + 2 * SLACK), :]
            r = win[SLACK : SLACK + CHUNK]
            cu[l, rows, :] = r * pltpu.roll(win, 1, 0)[SLACK : SLACK + CHUNK]
            cd[l, rows, :] = r * pltpu.roll(win, CHUNK + 2 * SLACK - 1, 0)[SLACK : SLACK + CHUNK]
            cl[l, rows, :] = r * pltpu.roll(r, 1, 1)
            cr[l, rows, :] = r * pltpu.roll(r, frame_cols - 1, 1)
            if l + 1 < layers:
                cv[l, rows, :] = r_ref[l + 1, rows, :] * r

    chunk_loop(count, body)


def explicit_step(src, dst, cu, cd, cl, cr, cv, s_ref):
    layers, frame_rows, frame_cols = dst.shape
    count = (frame_rows - 2 * SLACK) // CHUNK

    def body(c):
        lead = pl.multiple_of(c * CHUNK, 8)
        rows = pl.ds(pl.multiple_of(lead + SLACK, 8), CHUNK)
        for l in range(layers):
            win = src[l, pl.ds(lead, CHUNK + 2 * SLACK), :]
            f = win[SLACK : SLACK + CHUNK]
            up = pltpu.roll(win, 1, 0)[SLACK : SLACK + CHUNK]
            down = pltpu.roll(win, CHUNK + 2 * SLACK - 1, 0)[SLACK : SLACK + CHUNK]
            left = pltpu.roll(f, 1, 1)
            right = pltpu.roll(f, frame_cols - 1, 1)
            inflow = cu[l, rows, :] * (up - f)
            inflow = inflow + cd[l, rows, :] * (down - f)
            inflow = inflow + cl[l, rows, :] * (left - f)
            inflow = inflow + cr[l, rows, :] * (right - f)
            if l + 1 < layers:
                inflow = inflow + cv[l, rows, :] * (src[l + 1, rows, :] - f)
            if l > 0:
                inflow = inflow - cv[l - 1, rows, :] * (f - src[l - 1, rows, :])
            if l == layers - 1:
                inflow = inflow - AMBIENT_LOSS * f
            if l == 0 and s_ref is not None:
                inflow = inflow + s_ref[rows, :]
            dst[l, rows, :] = f + RATE * inflow

    chunk_loop(count, body)


def clear_slack(buf):
    layers, frame_rows, frame_cols = buf.shape
    zero = jnp.zeros((layers, SLACK, frame_cols), buf.dtype)
    buf[:, 0:SLACK, :] = zero
    buf[:, frame_rows - SLACK : frame_rows, :] = zero


def copy_center(src_view, dst_ref, height, breadth):
    def body(c):
        rows = pl.ds(pl.multiple_of(c * CHUNK, 8), CHUNK)
        from_rows = pl.ds(pl.multiple_of(c * CHUNK + SLACK + HALO, 8), CHUNK)
        dst_ref(rows, src_view(from_rows, breadth))

    chunk_loop(height // CHUNK, body)


def forward_kernel(f_ref, r_ref, s_ref, out_ref, cu, cd, cl, cr, cv, a, b):
    layers, height, breadth = out_ref.shape
    clear_slack(a)
    clear_slack(b)
    conductances(r_ref, cu, cd, cl, cr, cv)
    src = f_ref
    for index in range(STEPS):
        dst = a if index % 2 == 0 else b
        explicit_step(src, dst, cu, cd, cl, cr, cv, s_ref)
        src = dst

    def put(rows, value):
        out_ref[:, rows, :] = value

    copy_center(lambda rows, width: src[:, rows, 0:width], put, height, breadth)


def adjoint_kernel(a0_ref, r_ref, grad_ref, gsum_ref, cu, cd, cl, cr, cv, a, b):
    layers, height, breadth = grad_ref.shape
    a[...] = jnp.zeros(a.shape, a.dtype)
    clear_slack(b)
    a[0] = a0_ref[...]
    conductances(r_ref, cu, cd, cl, cr, cv)
    src = a
    for index in range(STEPS):
        view = src

        def put_sum(rows, value, first=(index == 0)):
            if first:
                gsum_ref[rows, :] = value
            else:
                gsum_ref[rows, :] = gsum_ref[rows, :] + value

        copy_center(lambda rows, width, v=view: v[0, rows, 0:width], put_sum, height, breadth)
        dst = b if index % 2 == 0 else a
        explicit_step(src, dst, cu, cd, cl, cr, cv, None)
        src = dst

    def put(rows, value):
        grad_ref[:, rows, :] = value

    copy_center(lambda rows, width: src[:, rows, 0:width], put, height, breadth)


def stencil_scratch(layers, frame_rows, frame_cols):
    whole = pltpu.VMEM((layers, frame_rows, frame_cols), jnp.float32)
    return [whole] * 4 + [pltpu.VMEM((layers - 1, frame_rows, frame_cols), jnp.float32), whole, whole]


def vmem_specs(count):
    return [pl.BlockSpec(memory_space=pltpu.VMEM) for _ in range(count)]


def run_forward(f_frame, r_frame, s_frame, height, breadth):
    layers, frame_rows, frame_cols = f_frame.shape
    return pl.pallas_call(
        forward_kernel,
        out_shape=jax.ShapeDtypeStruct((layers, height, breadth), jnp.float32),
        in_specs=vmem_specs(3),
        out_specs=vmem_specs(1)[0],
        scratch_shapes=stencil_scratch(layers, frame_rows, frame_cols),
        compiler_params=pltpu.CompilerParams(vmem_limit_bytes=56 * 1024 * 1024),
    )(f_frame, r_frame, s_frame)


def run_adjoint(a0_frame, r_frame, height, breadth):
    layers, frame_rows, frame_cols = r_frame.shape
    return pl.pallas_call(
        adjoint_kernel,
        out_shape=(
            jax.ShapeDtypeStruct((layers, height, breadth), jnp.float32),
            jax.ShapeDtypeStruct((height, breadth), jnp.float32),
        ),
        in_specs=vmem_specs(2),
        out_specs=tuple(vmem_specs(2)),
        scratch_shapes=stencil_scratch(layers, frame_rows, frame_cols),
        compiler_params=pltpu.CompilerParams(vmem_limit_bytes=56 * 1024 * 1024),
    )(a0_frame, r_frame)


def on_device(init_temp, power, die_owner, die_tile, classes, cond_table, target):
    row_count = lax.axis_size("row")
    col_count = lax.axis_size("col")
    devices_all = row_count * col_count
    layers, height, breadth = init_temp.shape
    tile_rows = height // TILE
    tile_cols = breadth // TILE
    die_count = power.shape[0]
    highest = lax.Precision.HIGHEST
    power_flat = power.reshape(die_count, TILE * TILE)
    owners = die_owner[:, 0]
    ordinal = jnp.arange(die_count, dtype=jnp.int32)
    same_owner = (owners[:, None] == owners[None, :]) & (ordinal[:, None] < ordinal[None, :])
    ranking = jnp.sum(same_owner.astype(jnp.int32), axis=0)
    slot_index = owners * CAP + ranking
    all_slots = jnp.arange(devices_all * CAP, dtype=jnp.int32)
    matched = all_slots[:, None] == slot_index[None, :]
    slot_die = jnp.sum(jnp.where(matched, ordinal[None, :] + 1, 0), axis=1) - 1
    slot_die = jnp.where(slot_die < 0, die_count, slot_die).reshape(devices_all, CAP)
    tile_column = jnp.zeros((die_count, LANE), jnp.float32).at[:, 0].set((die_tile + 1).astype(jnp.float32))
    payload = jnp.concatenate([power_flat, tile_column], 1)
    payload = jnp.concatenate([payload, jnp.zeros((1, payload.shape[1]), payload.dtype)], 0)
    outbound = jnp.take(payload, slot_die, axis=0)
    received = lax.all_to_all(outbound, ("row", "col"), split_axis=0, concat_axis=0, tiled=True)
    recv_tiles = received[:, :, TILE * TILE].astype(jnp.int32) - 1
    tile_range = jnp.arange(tile_rows * tile_cols, dtype=jnp.int32)
    recv_hot = (tile_range[:, None, None] == recv_tiles[None]).astype(jnp.float32)
    source_tiles = jnp.einsum("tdc,dcn->tn", recv_hot, received[:, :, : TILE * TILE], precision=highest)
    source = (
        source_tiles.reshape(tile_rows, tile_cols, TILE, TILE)
        .transpose(0, 2, 1, 3)
        .reshape(height, breadth)
    )
    root_cond = conduct_root(classes, cond_table)
    r_frame = framed(root_cond)
    s_frame = framed(source[None])[0]
    f_frame = framed(init_temp)
    heat_field = run_forward(f_frame, r_frame, s_frame, height, breadth)
    a0_frame = framed((heat_field[0] - target)[None])[0]
    adjoint, grad_sum = run_adjoint(a0_frame, r_frame, height, breadth)
    grad_tiles = (
        grad_sum.reshape(tile_rows, TILE, tile_cols, TILE)
        .transpose(0, 2, 1, 3)
        .reshape(tile_rows * tile_cols, TILE * TILE)
    )
    grad_tiles = jnp.concatenate([grad_tiles, jnp.zeros((1, grad_tiles.shape[1]), grad_tiles.dtype)], 0)
    tile_count = tile_rows * tile_cols
    backward = jnp.take(grad_tiles, jnp.where(recv_tiles < 0, tile_count, recv_tiles), axis=0)
    returned = lax.all_to_all(backward, ("row", "col"), split_axis=0, concat_axis=0, tiled=True)
    die_grad = (RATE * returned[owners, ranking]).reshape(die_count, TILE, TILE)
    return (heat_field, adjoint, die_grad)


def solution(mesh):
    in_specs = (
        P(None, "row", "col"),
        P(("row", "col"), None, None),
        P(("row", "col"), None),
        P(("row", "col")),
        P(None, "row", "col"),
        P(),
        P("row", "col"),
    )
    out_specs = (P(None, "row", "col"), P(None, "row", "col"), P(("row", "col"), None, None))
    return jax.shard_map(
        on_device, mesh=mesh, in_specs=in_specs, out_specs=out_specs, check_vma=False
    )
```

```python
import jax
import jax.numpy as jnp
from jax import lax
from jax.experimental import pallas as pl
from jax.experimental.pallas import tpu as pltpu
from jax.sharding import PartitionSpec as P

TILE = 64
CLASSES = 8
STEPS = 6
CAP = 2


RATE = 0.1
AMBIENT_LOSS = 0.3


def extended(cells, sides, width):
    for axis, dim in sides:
        count = lax.axis_size(axis)
        ends = count - 1
        head = lax.slice_in_dim(cells, 0, width, axis=dim)
        tail = lax.slice_in_dim(cells, cells.shape[dim] - width, cells.shape[dim], axis=dim)
        cells = jnp.concatenate(
            [
                lax.ppermute(tail, axis, [(i, (i + 1) % count) for i in range(ends)]),
                cells,
                lax.ppermute(head, axis, [((i + 1) % count, i) for i in range(ends)]),
            ],
            axis=dim,
        )
    return cells


def conduct_root(classes, cond_table):
    conduct = jnp.zeros(classes.shape, cond_table.dtype)
    for label in range(CLASSES):
        conduct = conduct + jnp.where(classes == label, cond_table[:, label][:, None, None], 0.0)
    return jnp.sqrt(conduct)


def advance(field, root_cond, source):
    middle = field[:, 1:-1, 1:-1]
    roots = root_cond[:, 1:-1, 1:-1]
    inflow = roots * root_cond[:, :-2, 1:-1] * (field[:, :-2, 1:-1] - middle)
    inflow = inflow + roots * root_cond[:, 2:, 1:-1] * (field[:, 2:, 1:-1] - middle)
    inflow = inflow + roots * root_cond[:, 1:-1, :-2] * (field[:, 1:-1, :-2] - middle)
    inflow = inflow + roots * root_cond[:, 1:-1, 2:] * (field[:, 1:-1, 2:] - middle)
    vertical = roots[1:] * roots[:-1] * (middle[1:] - middle[:-1])
    zero_layer = jnp.zeros_like(middle[:1])
    inflow = (
        inflow
        + jnp.concatenate([vertical, zero_layer], 0)
        - jnp.concatenate([zero_layer, vertical], 0)
    )
    inflow = inflow - AMBIENT_LOSS * jnp.concatenate([jnp.zeros_like(middle[:-1]), middle[-1:]], 0)
    if source is not None:
        inflow = inflow + jnp.concatenate([source[None], jnp.zeros_like(middle[1:])], 0)
    return middle + RATE * inflow


HALO = 16
SLACK = 8
CHUNK = 16
LANE = 128


def framed(cells):
    depth, height, breadth = cells.shape
    cols = lax.axis_size("col")
    rows = lax.axis_size("row")
    left = lax.ppermute(
        jnp.swapaxes(cells[:, :, breadth - HALO :], 1, 2), "col", [(i, i + 1) for i in range(cols - 1)]
    )
    right = lax.ppermute(jnp.swapaxes(cells[:, :, :HALO], 1, 2), "col", [(i + 1, i) for i in range(cols - 1)])
    left = jnp.swapaxes(left, 1, 2)
    right = jnp.swapaxes(right, 1, 2)
    gap = jnp.zeros((depth, height, LANE - 2 * HALO), cells.dtype)
    band = jnp.concatenate([cells, right, gap, left], axis=2)
    top = lax.ppermute(band[:, height - HALO :], "row", [(i, i + 1) for i in range(rows - 1)])
    bottom = lax.ppermute(band[:, :HALO], "row", [(i + 1, i) for i in range(rows - 1)])
    pad = jnp.zeros((depth, SLACK, band.shape[2]), cells.dtype)
    return jnp.concatenate([pad, top, band, bottom, pad], axis=1)


def chunk_loop(count, body):
    lax.fori_loop(0, count, lambda c, carry: (body(c), carry)[1], 0)


def conductances(r_ref, cu, cd, cl, cr, cv):
    layers, frame_rows, frame_cols = r_ref.shape
    count = (frame_rows - 2 * SLACK) // CHUNK

    def body(c):
        lead = pl.multiple_of(c * CHUNK, 8)
        rows = pl.ds(pl.multiple_of(lead + SLACK, 8), CHUNK)
        for l in range(layers):
            win = r_ref[l, pl.ds(lead, CHUNK + 2 * SLACK), :]
            r = win[SLACK : SLACK + CHUNK]
            cu[l, rows, :] = r * pltpu.roll(win, 1, 0)[SLACK : SLACK + CHUNK]
            cd[l, rows, :] = r * pltpu.roll(win, CHUNK + 2 * SLACK - 1, 0)[SLACK : SLACK + CHUNK]
            cl[l, rows, :] = r * pltpu.roll(r, 1, 1)
            cr[l, rows, :] = r * pltpu.roll(r, frame_cols - 1, 1)
            if l + 1 < layers:
                cv[l, rows, :] = r_ref[l + 1, rows, :] * r

    chunk_loop(count, body)


def explicit_step(src, dst, cu, cd, cl, cr, cv, s_ref):
    layers, frame_rows, frame_cols = dst.shape
    count = (frame_rows - 2 * SLACK) // CHUNK

    def body(c):
        lead = pl.multiple_of(c * CHUNK, 8)
        rows = pl.ds(pl.multiple_of(lead + SLACK, 8), CHUNK)
        for l in range(layers):
            win = src[l, pl.ds(lead, CHUNK + 2 * SLACK), :]
            f = win[SLACK : SLACK + CHUNK]
            up = pltpu.roll(win, 1, 0)[SLACK : SLACK + CHUNK]
            down = pltpu.roll(win, CHUNK + 2 * SLACK - 1, 0)[SLACK : SLACK + CHUNK]
            left = pltpu.roll(f, 1, 1)
            right = pltpu.roll(f, frame_cols - 1, 1)
            inflow = cu[l, rows, :] * (up - f)
            inflow = inflow + cd[l, rows, :] * (down - f)
            inflow = inflow + cl[l, rows, :] * (left - f)
            inflow = inflow + cr[l, rows, :] * (right - f)
            if l + 1 < layers:
                inflow = inflow + cv[l, rows, :] * (src[l + 1, rows, :] - f)
            if l > 0:
                inflow = inflow - cv[l - 1, rows, :] * (f - src[l - 1, rows, :])
            if l == layers - 1:
                inflow = inflow - AMBIENT_LOSS * f
            if l == 0 and s_ref is not None:
                inflow = inflow + s_ref[rows, :]
            dst[l, rows, :] = f + RATE * inflow

    chunk_loop(count, body)


def clear_slack(buf):
    layers, frame_rows, frame_cols = buf.shape
    zero = jnp.zeros((layers, SLACK, frame_cols), buf.dtype)
    buf[:, 0:SLACK, :] = zero
    buf[:, frame_rows - SLACK : frame_rows, :] = zero


def copy_center(src_view, dst_ref, height, breadth):
    def body(c):
        rows = pl.ds(pl.multiple_of(c * CHUNK, 8), CHUNK)
        from_rows = pl.ds(pl.multiple_of(c * CHUNK + SLACK + HALO, 8), CHUNK)
        dst_ref(rows, src_view(from_rows, breadth))

    chunk_loop(height // CHUNK, body)


def solve_kernel(f_ref, r_ref, s_ref, t_ref, out_ref, grad_ref, gsum_ref, cu, cd, cl, cr, cv, a, b):
    layers, height, breadth = out_ref.shape
    frame_rows = a.shape[1]
    clear_slack(a)
    clear_slack(b)
    conductances(r_ref, cu, cd, cl, cr, cv)
    src = f_ref
    for index in range(STEPS):
        dst = a if index % 2 == 0 else b
        explicit_step(src, dst, cu, cd, cl, cr, cv, s_ref)
        src = dst

    def put(rows, value):
        out_ref[:, rows, :] = value

    copy_center(lambda rows, width, v=src: v[:, rows, 0:width], put, height, breadth)
    final = src
    start = b if final is a else a
    start[1:] = jnp.zeros((layers - 1,) + start.shape[1:], start.dtype)

    def seed(c):
        rows = pl.ds(pl.multiple_of(c * CHUNK, 8), CHUNK)
        start[0, rows, :] = final[0, rows, :] - t_ref[rows, :]

    chunk_loop(frame_rows // CHUNK, seed)
    src = start
    for index in range(STEPS):
        view = src

        def put_sum(rows, value, first=(index == 0)):
            if first:
                gsum_ref[rows, :] = value
            else:
                gsum_ref[rows, :] = gsum_ref[rows, :] + value

        copy_center(lambda rows, width, v=view: v[0, rows, 0:width], put_sum, height, breadth)
        dst = final if src is start else start
        explicit_step(src, dst, cu, cd, cl, cr, cv, None)
        src = dst

    def put_grad(rows, value):
        grad_ref[:, rows, :] = value

    copy_center(lambda rows, width, v=src: v[:, rows, 0:width], put_grad, height, breadth)


def stencil_scratch(layers, frame_rows, frame_cols):
    whole = pltpu.VMEM((layers, frame_rows, frame_cols), jnp.float32)
    return [whole] * 4 + [pltpu.VMEM((layers - 1, frame_rows, frame_cols), jnp.float32), whole, whole]


def vmem_specs(count):
    return [pl.BlockSpec(memory_space=pltpu.VMEM) for _ in range(count)]


def run_solve(f_frame, r_frame, s_frame, t_frame, height, breadth):
    layers, frame_rows, frame_cols = f_frame.shape
    field = jax.ShapeDtypeStruct((layers, height, breadth), jnp.float32)
    return pl.pallas_call(
        solve_kernel,
        out_shape=(field, field, jax.ShapeDtypeStruct((height, breadth), jnp.float32)),
        in_specs=vmem_specs(4),
        out_specs=tuple(vmem_specs(3)),
        scratch_shapes=stencil_scratch(layers, frame_rows, frame_cols),
        compiler_params=pltpu.CompilerParams(vmem_limit_bytes=60 * 1024 * 1024),
    )(f_frame, r_frame, s_frame, t_frame)


def send_dies(outbound, row_count, col_count):
    received = lax.all_to_all(
        outbound.reshape(row_count * col_count, CAP, -1),
        ("row", "col"),
        split_axis=0,
        concat_axis=0,
        tiled=True,
    )
    return received.reshape(row_count * col_count * CAP, -1)


def return_grads(backward, row_count, col_count):
    returned = lax.all_to_all(
        backward.reshape(row_count * col_count, CAP, -1),
        ("row", "col"),
        split_axis=0,
        concat_axis=0,
        tiled=True,
    )
    return returned.reshape(row_count * col_count * CAP, -1)


def on_device(init_temp, power, die_owner, die_tile, classes, cond_table, target):
    row_count = lax.axis_size("row")
    col_count = lax.axis_size("col")
    devices_all = row_count * col_count
    layers, height, breadth = init_temp.shape
    tile_rows = height // TILE
    tile_cols = breadth // TILE
    die_count = power.shape[0]
    highest = lax.Precision.HIGHEST
    power_flat = power.reshape(die_count, TILE * TILE)
    owners = die_owner[:, 0]
    ordinal = jnp.arange(die_count, dtype=jnp.int32)
    same_owner = (owners[:, None] == owners[None, :]) & (ordinal[:, None] < ordinal[None, :])
    ranking = jnp.sum(same_owner.astype(jnp.int32), axis=0)
    slot_index = owners * CAP + ranking
    all_slots = jnp.arange(devices_all * CAP, dtype=jnp.int32)
    matched = all_slots[:, None] == slot_index[None, :]
    send_hot = matched.astype(jnp.float32)
    tile_column = jnp.zeros((die_count, LANE), jnp.float32).at[:, 0].set((die_tile + 1).astype(jnp.float32))
    outbound = jnp.dot(send_hot, jnp.concatenate([power_flat, tile_column], 1), precision=highest)
    received = send_dies(outbound, row_count, col_count)
    recv_tiles = received[:, TILE * TILE].astype(jnp.int32) - 1
    received = received[:, : TILE * TILE]
    tile_range = jnp.arange(tile_rows * tile_cols, dtype=jnp.int32)
    recv_hot = (tile_range[:, None] == recv_tiles[None, :]).astype(jnp.float32)
    source_tiles = jnp.dot(recv_hot, received, precision=highest)
    source = (
        source_tiles.reshape(tile_rows, tile_cols, TILE, TILE)
        .transpose(0, 2, 1, 3)
        .reshape(height, breadth)
    )
    root_cond = conduct_root(classes, cond_table)
    r_frame = framed(root_cond)
    s_frame = framed(source[None])[0]
    f_frame = framed(init_temp)
    t_frame = framed(target[None])[0]
    heat_field, adjoint, grad_sum = run_solve(f_frame, r_frame, s_frame, t_frame, height, breadth)
    grad_tiles = (
        grad_sum.reshape(tile_rows, TILE, tile_cols, TILE)
        .transpose(0, 2, 1, 3)
        .reshape(tile_rows * tile_cols, TILE * TILE)
    )
    backward = jnp.dot(recv_hot.T, grad_tiles, precision=highest)
    returned = return_grads(backward, row_count, col_count)
    die_grad = (RATE * jnp.dot(send_hot.T, returned, precision=highest)).reshape(
        die_count, TILE, TILE
    )
    return (heat_field, adjoint, die_grad)


def solution(mesh):
    in_specs = (
        P(None, "row", "col"),
        P(("row", "col"), None, None),
        P(("row", "col"), None),
        P(("row", "col")),
        P(None, "row", "col"),
        P(),
        P("row", "col"),
    )
    out_specs = (P(None, "row", "col"), P(None, "row", "col"), P(("row", "col"), None, None))
    return jax.shard_map(
        on_device, mesh=mesh, in_specs=in_specs, out_specs=out_specs, check_vma=False
    )
```

```python
import jax
import jax.numpy as jnp
from jax import lax
from jax.experimental import pallas as pl
from jax.experimental.pallas import tpu as pltpu
from jax.sharding import PartitionSpec as P

TILE = 64
CLASSES = 8
STEPS = 6
CAP = 2


RATE = 0.1
AMBIENT_LOSS = 0.3


def extended(cells, sides, width):
    for axis, dim in sides:
        count = lax.axis_size(axis)
        ends = count - 1
        head = lax.slice_in_dim(cells, 0, width, axis=dim)
        tail = lax.slice_in_dim(cells, cells.shape[dim] - width, cells.shape[dim], axis=dim)
        cells = jnp.concatenate(
            [
                lax.ppermute(tail, axis, [(i, (i + 1) % count) for i in range(ends)]),
                cells,
                lax.ppermute(head, axis, [((i + 1) % count, i) for i in range(ends)]),
            ],
            axis=dim,
        )
    return cells


def conduct_root(classes, cond_table):
    conduct = jnp.zeros(classes.shape, cond_table.dtype)
    for label in range(CLASSES):
        conduct = conduct + jnp.where(classes == label, cond_table[:, label][:, None, None], 0.0)
    return jnp.sqrt(conduct)


def advance(field, root_cond, source):
    middle = field[:, 1:-1, 1:-1]
    roots = root_cond[:, 1:-1, 1:-1]
    inflow = roots * root_cond[:, :-2, 1:-1] * (field[:, :-2, 1:-1] - middle)
    inflow = inflow + roots * root_cond[:, 2:, 1:-1] * (field[:, 2:, 1:-1] - middle)
    inflow = inflow + roots * root_cond[:, 1:-1, :-2] * (field[:, 1:-1, :-2] - middle)
    inflow = inflow + roots * root_cond[:, 1:-1, 2:] * (field[:, 1:-1, 2:] - middle)
    vertical = roots[1:] * roots[:-1] * (middle[1:] - middle[:-1])
    zero_layer = jnp.zeros_like(middle[:1])
    inflow = (
        inflow
        + jnp.concatenate([vertical, zero_layer], 0)
        - jnp.concatenate([zero_layer, vertical], 0)
    )
    inflow = inflow - AMBIENT_LOSS * jnp.concatenate([jnp.zeros_like(middle[:-1]), middle[-1:]], 0)
    if source is not None:
        inflow = inflow + jnp.concatenate([source[None], jnp.zeros_like(middle[1:])], 0)
    return middle + RATE * inflow


HALO = 16
SLACK = 8
CHUNK = 16
LANE = 128


def framed(cells):
    depth, height, breadth = cells.shape
    cols = lax.axis_size("col")
    rows = lax.axis_size("row")
    left = lax.ppermute(
        jnp.swapaxes(cells[:, :, breadth - HALO :], 1, 2), "col", [(i, i + 1) for i in range(cols - 1)]
    )
    right = lax.ppermute(jnp.swapaxes(cells[:, :, :HALO], 1, 2), "col", [(i + 1, i) for i in range(cols - 1)])
    left = jnp.swapaxes(left, 1, 2)
    right = jnp.swapaxes(right, 1, 2)
    gap = jnp.zeros((depth, height, LANE - 2 * HALO), cells.dtype)
    band = jnp.concatenate([cells, right, gap, left], axis=2)
    top = lax.ppermute(band[:, height - HALO :], "row", [(i, i + 1) for i in range(rows - 1)])
    bottom = lax.ppermute(band[:, :HALO], "row", [(i + 1, i) for i in range(rows - 1)])
    pad = jnp.zeros((depth, SLACK, band.shape[2]), cells.dtype)
    return jnp.concatenate([pad, top, band, bottom, pad], axis=1)


def chunk_loop(count, body):
    lax.fori_loop(0, count, lambda c, carry: (body(c), carry)[1], 0)


def conductances(r_ref, cu, cd, cl, cr, dg, cv):
    layers, frame_rows, frame_cols = r_ref.shape
    count = (frame_rows - 2 * SLACK) // CHUNK

    def body(c):
        lead = pl.multiple_of(c * CHUNK, 8)
        rows = pl.ds(pl.multiple_of(lead + SLACK, 8), CHUNK)
        below = None
        for l in range(layers):
            win = r_ref[l, pl.ds(lead, CHUNK + 2 * SLACK), :]
            r = win[SLACK : SLACK + CHUNK]
            up = r * pltpu.roll(win, 1, 0)[SLACK : SLACK + CHUNK]
            down = r * pltpu.roll(win, CHUNK + 2 * SLACK - 1, 0)[SLACK : SLACK + CHUNK]
            left = r * pltpu.roll(r, 1, 1)
            right = r * pltpu.roll(r, frame_cols - 1, 1)
            total = up + down + left + right
            cu[l, rows, :] = RATE * up
            cd[l, rows, :] = RATE * down
            cl[l, rows, :] = RATE * left
            cr[l, rows, :] = RATE * right
            if l + 1 < layers:
                vertical = r_ref[l + 1, rows, :] * r
                cv[l, rows, :] = RATE * vertical
                total = total + vertical
            if below is not None:
                total = total + below
            if l == layers - 1:
                total = total + AMBIENT_LOSS
            dg[l, rows, :] = 1.0 - RATE * total
            below = vertical if l + 1 < layers else None

    chunk_loop(count, body)


def explicit_step(src, dst, cu, cd, cl, cr, dg, cv, s_ref):
    layers, frame_rows, frame_cols = dst.shape
    count = (frame_rows - 2 * SLACK) // CHUNK

    def body(c):
        lead = pl.multiple_of(c * CHUNK, 8)
        rows = pl.ds(pl.multiple_of(lead + SLACK, 8), CHUNK)
        for l in range(layers):
            win = src[l, pl.ds(lead, CHUNK + 2 * SLACK), :]
            f = win[SLACK : SLACK + CHUNK]
            up = pltpu.roll(win, 1, 0)[SLACK : SLACK + CHUNK]
            down = pltpu.roll(win, CHUNK + 2 * SLACK - 1, 0)[SLACK : SLACK + CHUNK]
            left = pltpu.roll(f, 1, 1)
            right = pltpu.roll(f, frame_cols - 1, 1)
            value = dg[l, rows, :] * f + cu[l, rows, :] * up
            value = value + cd[l, rows, :] * down
            value = value + cl[l, rows, :] * left
            value = value + cr[l, rows, :] * right
            if l + 1 < layers:
                value = value + cv[l, rows, :] * src[l + 1, rows, :]
            if l > 0:
                value = value + cv[l - 1, rows, :] * src[l - 1, rows, :]
            if l == 0 and s_ref is not None:
                value = value + RATE * s_ref[rows, :]
            dst[l, rows, :] = value

    chunk_loop(count, body)


def clear_slack(buf):
    layers, frame_rows, frame_cols = buf.shape
    zero = jnp.zeros((layers, SLACK, frame_cols), buf.dtype)
    buf[:, 0:SLACK, :] = zero
    buf[:, frame_rows - SLACK : frame_rows, :] = zero


def copy_center(src_view, dst_ref, height, breadth):
    def body(c):
        rows = pl.ds(pl.multiple_of(c * CHUNK, 8), CHUNK)
        from_rows = pl.ds(pl.multiple_of(c * CHUNK + SLACK + HALO, 8), CHUNK)
        dst_ref(rows, src_view(from_rows, breadth))

    chunk_loop(height // CHUNK, body)


def solve_kernel(f_ref, r_ref, s_ref, t_ref, out_ref, grad_ref, gsum_ref, cu, cd, cl, cr, dg, cv, a, b):
    layers, height, breadth = out_ref.shape
    frame_rows = a.shape[1]
    clear_slack(a)
    clear_slack(b)
    conductances(r_ref, cu, cd, cl, cr, dg, cv)
    src = f_ref
    for index in range(STEPS):
        dst = a if index % 2 == 0 else b
        explicit_step(src, dst, cu, cd, cl, cr, dg, cv, s_ref)
        src = dst

    def put(rows, value):
        out_ref[:, rows, :] = value

    copy_center(lambda rows, width, v=src: v[:, rows, 0:width], put, height, breadth)
    final = src
    start = b if final is a else a
    start[1:] = jnp.zeros((layers - 1,) + start.shape[1:], start.dtype)

    def seed(c):
        rows = pl.ds(pl.multiple_of(c * CHUNK, 8), CHUNK)
        start[0, rows, :] = final[0, rows, :] - t_ref[rows, :]

    chunk_loop(frame_rows // CHUNK, seed)
    src = start
    for index in range(STEPS):
        view = src

        def put_sum(rows, value, first=(index == 0)):
            if first:
                gsum_ref[rows, :] = value
            else:
                gsum_ref[rows, :] = gsum_ref[rows, :] + value

        copy_center(lambda rows, width, v=view: v[0, rows, 0:width], put_sum, height, breadth)
        dst = final if src is start else start
        explicit_step(src, dst, cu, cd, cl, cr, dg, cv, None)
        src = dst

    def put_grad(rows, value):
        grad_ref[:, rows, :] = value

    copy_center(lambda rows, width, v=src: v[:, rows, 0:width], put_grad, height, breadth)


def stencil_scratch(layers, frame_rows, frame_cols):
    whole = pltpu.VMEM((layers, frame_rows, frame_cols), jnp.float32)
    return [whole] * 5 + [pltpu.VMEM((layers - 1, frame_rows, frame_cols), jnp.float32), whole, whole]


def vmem_specs(count):
    return [pl.BlockSpec(memory_space=pltpu.VMEM) for _ in range(count)]


def run_solve(f_frame, r_frame, s_frame, t_frame, height, breadth):
    layers, frame_rows, frame_cols = f_frame.shape
    field = jax.ShapeDtypeStruct((layers, height, breadth), jnp.float32)
    return pl.pallas_call(
        solve_kernel,
        out_shape=(field, field, jax.ShapeDtypeStruct((height, breadth), jnp.float32)),
        in_specs=vmem_specs(4),
        out_specs=tuple(vmem_specs(3)),
        scratch_shapes=stencil_scratch(layers, frame_rows, frame_cols),
        compiler_params=pltpu.CompilerParams(vmem_limit_bytes=60 * 1024 * 1024),
    )(f_frame, r_frame, s_frame, t_frame)


def send_dies(outbound, row_count, col_count):
    received = lax.all_to_all(
        outbound.reshape(row_count * col_count, CAP, -1),
        ("row", "col"),
        split_axis=0,
        concat_axis=0,
        tiled=True,
    )
    return received.reshape(row_count * col_count * CAP, -1)


def return_grads(backward, row_count, col_count):
    returned = lax.all_to_all(
        backward.reshape(row_count * col_count, CAP, -1),
        ("row", "col"),
        split_axis=0,
        concat_axis=0,
        tiled=True,
    )
    return returned.reshape(row_count * col_count * CAP, -1)


def on_device(init_temp, power, die_owner, die_tile, classes, cond_table, target):
    row_count = lax.axis_size("row")
    col_count = lax.axis_size("col")
    devices_all = row_count * col_count
    layers, height, breadth = init_temp.shape
    tile_rows = height // TILE
    tile_cols = breadth // TILE
    die_count = power.shape[0]
    highest = lax.Precision.HIGHEST
    power_flat = power.reshape(die_count, TILE * TILE)
    owners = die_owner[:, 0]
    ordinal = jnp.arange(die_count, dtype=jnp.int32)
    same_owner = (owners[:, None] == owners[None, :]) & (ordinal[:, None] < ordinal[None, :])
    ranking = jnp.sum(same_owner.astype(jnp.int32), axis=0)
    slot_index = owners * CAP + ranking
    all_slots = jnp.arange(devices_all * CAP, dtype=jnp.int32)
    matched = all_slots[:, None] == slot_index[None, :]
    send_hot = matched.astype(jnp.float32)
    tile_column = jnp.zeros((die_count, LANE), jnp.float32).at[:, 0].set((die_tile + 1).astype(jnp.float32))
    outbound = jnp.dot(send_hot, jnp.concatenate([power_flat, tile_column], 1), precision=highest)
    received = send_dies(outbound, row_count, col_count)
    recv_tiles = received[:, TILE * TILE].astype(jnp.int32) - 1
    received = received[:, : TILE * TILE]
    tile_range = jnp.arange(tile_rows * tile_cols, dtype=jnp.int32)
    recv_hot = (tile_range[:, None] == recv_tiles[None, :]).astype(jnp.float32)
    source_tiles = jnp.dot(recv_hot, received, precision=highest)
    source = (
        source_tiles.reshape(tile_rows, tile_cols, TILE, TILE)
        .transpose(0, 2, 1, 3)
        .reshape(height, breadth)
    )
    root_cond = conduct_root(classes, cond_table)
    r_frame = framed(root_cond)
    s_frame = framed(source[None])[0]
    f_frame = framed(init_temp)
    t_frame = framed(target[None])[0]
    heat_field, adjoint, grad_sum = run_solve(f_frame, r_frame, s_frame, t_frame, height, breadth)
    grad_tiles = (
        grad_sum.reshape(tile_rows, TILE, tile_cols, TILE)
        .transpose(0, 2, 1, 3)
        .reshape(tile_rows * tile_cols, TILE * TILE)
    )
    backward = jnp.dot(recv_hot.T, grad_tiles, precision=highest)
    returned = return_grads(backward, row_count, col_count)
    die_grad = (RATE * jnp.dot(send_hot.T, returned, precision=highest)).reshape(
        die_count, TILE, TILE
    )
    return (heat_field, adjoint, die_grad)


def solution(mesh):
    in_specs = (
        P(None, "row", "col"),
        P(("row", "col"), None, None),
        P(("row", "col"), None),
        P(("row", "col")),
        P(None, "row", "col"),
        P(),
        P("row", "col"),
    )
    out_specs = (P(None, "row", "col"), P(None, "row", "col"), P(("row", "col"), None, None))
    return jax.shard_map(
        on_device, mesh=mesh, in_specs=in_specs, out_specs=out_specs, check_vma=False
    )
```

```python
import jax
import jax.numpy as jnp
from jax import lax
from jax.experimental import pallas as pl
from jax.experimental.pallas import tpu as pltpu
from jax.sharding import PartitionSpec as P

TILE = 64
CLASSES = 8
STEPS = 6
CAP = 2


RATE = 0.1
AMBIENT_LOSS = 0.3


def extended(cells, sides, width):
    for axis, dim in sides:
        count = lax.axis_size(axis)
        ends = count - 1
        head = lax.slice_in_dim(cells, 0, width, axis=dim)
        tail = lax.slice_in_dim(cells, cells.shape[dim] - width, cells.shape[dim], axis=dim)
        cells = jnp.concatenate(
            [
                lax.ppermute(tail, axis, [(i, (i + 1) % count) for i in range(ends)]),
                cells,
                lax.ppermute(head, axis, [((i + 1) % count, i) for i in range(ends)]),
            ],
            axis=dim,
        )
    return cells


def conduct_root(classes, cond_table):
    conduct = jnp.zeros(classes.shape, cond_table.dtype)
    for label in range(CLASSES):
        conduct = conduct + jnp.where(classes == label, cond_table[:, label][:, None, None], 0.0)
    return jnp.sqrt(conduct)


def advance(field, root_cond, source):
    middle = field[:, 1:-1, 1:-1]
    roots = root_cond[:, 1:-1, 1:-1]
    inflow = roots * root_cond[:, :-2, 1:-1] * (field[:, :-2, 1:-1] - middle)
    inflow = inflow + roots * root_cond[:, 2:, 1:-1] * (field[:, 2:, 1:-1] - middle)
    inflow = inflow + roots * root_cond[:, 1:-1, :-2] * (field[:, 1:-1, :-2] - middle)
    inflow = inflow + roots * root_cond[:, 1:-1, 2:] * (field[:, 1:-1, 2:] - middle)
    vertical = roots[1:] * roots[:-1] * (middle[1:] - middle[:-1])
    zero_layer = jnp.zeros_like(middle[:1])
    inflow = (
        inflow
        + jnp.concatenate([vertical, zero_layer], 0)
        - jnp.concatenate([zero_layer, vertical], 0)
    )
    inflow = inflow - AMBIENT_LOSS * jnp.concatenate([jnp.zeros_like(middle[:-1]), middle[-1:]], 0)
    if source is not None:
        inflow = inflow + jnp.concatenate([source[None], jnp.zeros_like(middle[1:])], 0)
    return middle + RATE * inflow


HALO = 16
SLACK = 8
CHUNK = 8
LANE = 128


def framed(cells):
    depth, height, breadth = cells.shape
    cols = lax.axis_size("col")
    rows = lax.axis_size("row")
    left = lax.ppermute(
        jnp.swapaxes(cells[:, :, breadth - HALO :], 1, 2), "col", [(i, i + 1) for i in range(cols - 1)]
    )
    right = lax.ppermute(jnp.swapaxes(cells[:, :, :HALO], 1, 2), "col", [(i + 1, i) for i in range(cols - 1)])
    left = jnp.swapaxes(left, 1, 2)
    right = jnp.swapaxes(right, 1, 2)
    gap = jnp.zeros((depth, height, LANE - 2 * HALO), cells.dtype)
    band = jnp.concatenate([cells, right, gap, left], axis=2)
    top = lax.ppermute(band[:, height - HALO :], "row", [(i, i + 1) for i in range(rows - 1)])
    bottom = lax.ppermute(band[:, :HALO], "row", [(i + 1, i) for i in range(rows - 1)])
    pad = jnp.zeros((depth, SLACK, band.shape[2]), cells.dtype)
    return jnp.concatenate([pad, top, band, bottom, pad], axis=1)


def chunk_loop(count, body):
    lax.fori_loop(0, count, lambda c, carry: (body(c), carry)[1], 0, unroll=9)


def conductances(r_ref, cu, cd, cl, cr, dg, cv):
    layers, frame_rows, frame_cols = r_ref.shape
    count = (frame_rows - 2 * SLACK) // CHUNK

    def body(c):
        lead = pl.multiple_of(c * CHUNK, 8)
        rows = pl.ds(pl.multiple_of(lead + SLACK, 8), CHUNK)
        below = None
        for l in range(layers):
            win = r_ref[l, pl.ds(lead, CHUNK + 2 * SLACK), :]
            r = win[SLACK : SLACK + CHUNK]
            up = r * pltpu.roll(win, 1, 0)[SLACK : SLACK + CHUNK]
            down = r * pltpu.roll(win, CHUNK + 2 * SLACK - 1, 0)[SLACK : SLACK + CHUNK]
            left = r * pltpu.roll(r, 1, 1)
            right = r * pltpu.roll(r, frame_cols - 1, 1)
            total = up + down + left + right
            cu[l, rows, :] = RATE * up
            cd[l, rows, :] = RATE * down
            cl[l, rows, :] = RATE * left
            cr[l, rows, :] = RATE * right
            if l + 1 < layers:
                vertical = r_ref[l + 1, rows, :] * r
                cv[l, rows, :] = RATE * vertical
                total = total + vertical
            if below is not None:
                total = total + below
            if l == layers - 1:
                total = total + AMBIENT_LOSS
            dg[l, rows, :] = 1.0 - RATE * total
            below = vertical if l + 1 < layers else None

    chunk_loop(count, body)


def explicit_step(src, dst, cu, cd, cl, cr, dg, cv, s_ref):
    layers, frame_rows, frame_cols = dst.shape
    count = (frame_rows - 2 * SLACK) // CHUNK

    def body(c):
        lead = pl.multiple_of(c * CHUNK, 8)
        rows = pl.ds(pl.multiple_of(lead + SLACK, 8), CHUNK)
        above = pl.ds(pl.multiple_of(lead + SLACK - 8, 8), 8)
        below = pl.ds(pl.multiple_of(lead + SLACK + CHUNK, 8), 8)
        centre = [src[0, rows, :]] + [None] * (layers - 1)
        lower = None
        for l in range(layers):
            f = centre[l]
            win = jnp.concatenate([src[l, above, :], f, src[l, below, :]], axis=0)
            size = win.shape[0]
            up = pltpu.roll(win, 1, 0)[8 : 8 + CHUNK]
            down = pltpu.roll(win, size - 1, 0)[8 : 8 + CHUNK]
            left = pltpu.roll(f, 1, 1)
            right = pltpu.roll(f, frame_cols - 1, 1)
            value = dg[l, rows, :] * f + cu[l, rows, :] * up
            value = value + cd[l, rows, :] * down
            value = value + cl[l, rows, :] * left
            value = value + cr[l, rows, :] * right
            upper = None
            if l + 1 < layers:
                centre[l + 1] = src[l + 1, rows, :]
                upper = cv[l, rows, :]
                value = value + upper * centre[l + 1]
            if l > 0:
                value = value + lower * centre[l - 1]
            if l == 0 and s_ref is not None:
                value = value + RATE * s_ref[rows, :]
            dst[l, rows, :] = value
            lower = upper

    chunk_loop(count, body)


def clear_slack(buf):
    layers, frame_rows, frame_cols = buf.shape
    zero = jnp.zeros((layers, SLACK, frame_cols), buf.dtype)
    buf[:, 0:SLACK, :] = zero
    buf[:, frame_rows - SLACK : frame_rows, :] = zero


def copy_center(src_view, dst_ref, height, breadth):
    def body(c):
        rows = pl.ds(pl.multiple_of(c * CHUNK, 8), CHUNK)
        from_rows = pl.ds(pl.multiple_of(c * CHUNK + SLACK + HALO, 8), CHUNK)
        dst_ref(rows, src_view(from_rows, breadth))

    chunk_loop(height // CHUNK, body)


def solve_kernel(f_ref, r_ref, s_ref, t_ref, out_ref, grad_ref, gsum_ref, cu, cd, cl, cr, dg, cv, a, b):
    layers, height, breadth = out_ref.shape
    frame_rows = a.shape[1]
    clear_slack(a)
    clear_slack(b)
    conductances(r_ref, cu, cd, cl, cr, dg, cv)
    src = f_ref
    for index in range(STEPS):
        dst = a if index % 2 == 0 else b
        explicit_step(src, dst, cu, cd, cl, cr, dg, cv, s_ref)
        src = dst

    def put(rows, value):
        out_ref[:, rows, :] = value

    copy_center(lambda rows, width, v=src: v[:, rows, 0:width], put, height, breadth)
    final = src
    start = b if final is a else a
    start[1:] = jnp.zeros((layers - 1,) + start.shape[1:], start.dtype)

    def seed(c):
        rows = pl.ds(pl.multiple_of(c * CHUNK, 8), CHUNK)
        start[0, rows, :] = final[0, rows, :] - t_ref[rows, :]

    chunk_loop(frame_rows // CHUNK, seed)
    src = start
    for index in range(STEPS):
        view = src

        def put_sum(rows, value, first=(index == 0)):
            if first:
                gsum_ref[rows, :] = value
            else:
                gsum_ref[rows, :] = gsum_ref[rows, :] + value

        copy_center(lambda rows, width, v=view: v[0, rows, 0:width], put_sum, height, breadth)
        dst = final if src is start else start
        explicit_step(src, dst, cu, cd, cl, cr, dg, cv, None)
        src = dst

    def put_grad(rows, value):
        grad_ref[:, rows, :] = value

    copy_center(lambda rows, width, v=src: v[:, rows, 0:width], put_grad, height, breadth)


def stencil_scratch(layers, frame_rows, frame_cols):
    whole = pltpu.VMEM((layers, frame_rows, frame_cols), jnp.float32)
    return [whole] * 5 + [pltpu.VMEM((layers - 1, frame_rows, frame_cols), jnp.float32), whole, whole]


def vmem_specs(count):
    return [pl.BlockSpec(memory_space=pltpu.VMEM) for _ in range(count)]


def run_solve(f_frame, r_frame, s_frame, t_frame, height, breadth):
    layers, frame_rows, frame_cols = f_frame.shape
    field = jax.ShapeDtypeStruct((layers, height, breadth), jnp.float32)
    return pl.pallas_call(
        solve_kernel,
        out_shape=(field, field, jax.ShapeDtypeStruct((height, breadth), jnp.float32)),
        in_specs=vmem_specs(4),
        out_specs=tuple(vmem_specs(3)),
        scratch_shapes=stencil_scratch(layers, frame_rows, frame_cols),
        compiler_params=pltpu.CompilerParams(vmem_limit_bytes=60 * 1024 * 1024),
    )(f_frame, r_frame, s_frame, t_frame)


def send_dies(outbound, row_count, col_count):
    received = lax.all_to_all(
        outbound.reshape(row_count * col_count, CAP, -1),
        ("row", "col"),
        split_axis=0,
        concat_axis=0,
        tiled=True,
    )
    return received.reshape(row_count * col_count * CAP, -1)


def return_grads(backward, row_count, col_count):
    returned = lax.all_to_all(
        backward.reshape(row_count * col_count, CAP, -1),
        ("row", "col"),
        split_axis=0,
        concat_axis=0,
        tiled=True,
    )
    return returned.reshape(row_count * col_count * CAP, -1)


def on_device(init_temp, power, die_owner, die_tile, classes, cond_table, target):
    row_count = lax.axis_size("row")
    col_count = lax.axis_size("col")
    devices_all = row_count * col_count
    layers, height, breadth = init_temp.shape
    tile_rows = height // TILE
    tile_cols = breadth // TILE
    die_count = power.shape[0]
    highest = lax.Precision.HIGHEST
    power_flat = power.reshape(die_count, TILE * TILE)
    owners = die_owner[:, 0]
    ordinal = jnp.arange(die_count, dtype=jnp.int32)
    same_owner = (owners[:, None] == owners[None, :]) & (ordinal[:, None] < ordinal[None, :])
    ranking = jnp.sum(same_owner.astype(jnp.int32), axis=0)
    slot_index = owners * CAP + ranking
    all_slots = jnp.arange(devices_all * CAP, dtype=jnp.int32)
    matched = all_slots[:, None] == slot_index[None, :]
    send_hot = matched.astype(jnp.float32)
    tile_column = jnp.zeros((die_count, LANE), jnp.float32).at[:, 0].set((die_tile + 1).astype(jnp.float32))
    outbound = jnp.dot(send_hot, jnp.concatenate([power_flat, tile_column], 1), precision=highest)
    received = send_dies(outbound, row_count, col_count)
    recv_tiles = received[:, TILE * TILE].astype(jnp.int32) - 1
    received = received[:, : TILE * TILE]
    tile_range = jnp.arange(tile_rows * tile_cols, dtype=jnp.int32)
    recv_hot = (tile_range[:, None] == recv_tiles[None, :]).astype(jnp.float32)
    source_tiles = jnp.dot(recv_hot, received, precision=highest)
    source = (
        source_tiles.reshape(tile_rows, tile_cols, TILE, TILE)
        .transpose(0, 2, 1, 3)
        .reshape(height, breadth)
    )
    root_cond = conduct_root(classes, cond_table)
    r_frame = framed(root_cond)
    s_frame = framed(source[None])[0]
    f_frame = framed(init_temp)
    t_frame = framed(target[None])[0]
    heat_field, adjoint, grad_sum = run_solve(f_frame, r_frame, s_frame, t_frame, height, breadth)
    grad_tiles = (
        grad_sum.reshape(tile_rows, TILE, tile_cols, TILE)
        .transpose(0, 2, 1, 3)
        .reshape(tile_rows * tile_cols, TILE * TILE)
    )
    backward = jnp.dot(recv_hot.T, grad_tiles, precision=highest)
    returned = return_grads(backward, row_count, col_count)
    die_grad = (RATE * jnp.dot(send_hot.T, returned, precision=highest)).reshape(
        die_count, TILE, TILE
    )
    return (heat_field, adjoint, die_grad)


def solution(mesh):
    in_specs = (
        P(None, "row", "col"),
        P(("row", "col"), None, None),
        P(("row", "col"), None),
        P(("row", "col")),
        P(None, "row", "col"),
        P(),
        P("row", "col"),
    )
    out_specs = (P(None, "row", "col"), P(None, "row", "col"), P(("row", "col"), None, None))
    return jax.shard_map(
        on_device, mesh=mesh, in_specs=in_specs, out_specs=out_specs, check_vma=False
    )
```

```python
import jax
import jax.numpy as jnp
from jax import lax
from jax.experimental import pallas as pl
from jax.experimental.pallas import tpu as pltpu
from jax.sharding import PartitionSpec as P

TILE = 64
CLASSES = 8
STEPS = 6
CAP = 2


RATE = 0.1
AMBIENT_LOSS = 0.3


def extended(cells, sides, width):
    for axis, dim in sides:
        count = lax.axis_size(axis)
        ends = count - 1
        head = lax.slice_in_dim(cells, 0, width, axis=dim)
        tail = lax.slice_in_dim(cells, cells.shape[dim] - width, cells.shape[dim], axis=dim)
        cells = jnp.concatenate(
            [
                lax.ppermute(tail, axis, [(i, (i + 1) % count) for i in range(ends)]),
                cells,
                lax.ppermute(head, axis, [((i + 1) % count, i) for i in range(ends)]),
            ],
            axis=dim,
        )
    return cells


def conduct_root(classes, cond_table):
    conduct = jnp.zeros(classes.shape, cond_table.dtype)
    for label in range(CLASSES):
        conduct = conduct + jnp.where(classes == label, cond_table[:, label][:, None, None], 0.0)
    return jnp.sqrt(conduct)


def advance(field, root_cond, source):
    middle = field[:, 1:-1, 1:-1]
    roots = root_cond[:, 1:-1, 1:-1]
    inflow = roots * root_cond[:, :-2, 1:-1] * (field[:, :-2, 1:-1] - middle)
    inflow = inflow + roots * root_cond[:, 2:, 1:-1] * (field[:, 2:, 1:-1] - middle)
    inflow = inflow + roots * root_cond[:, 1:-1, :-2] * (field[:, 1:-1, :-2] - middle)
    inflow = inflow + roots * root_cond[:, 1:-1, 2:] * (field[:, 1:-1, 2:] - middle)
    vertical = roots[1:] * roots[:-1] * (middle[1:] - middle[:-1])
    zero_layer = jnp.zeros_like(middle[:1])
    inflow = (
        inflow
        + jnp.concatenate([vertical, zero_layer], 0)
        - jnp.concatenate([zero_layer, vertical], 0)
    )
    inflow = inflow - AMBIENT_LOSS * jnp.concatenate([jnp.zeros_like(middle[:-1]), middle[-1:]], 0)
    if source is not None:
        inflow = inflow + jnp.concatenate([source[None], jnp.zeros_like(middle[1:])], 0)
    return middle + RATE * inflow


HALO = 16
SLACK = 8
CHUNK = 8
LANE = 128


def framed(cells):
    depth, height, breadth = cells.shape
    cols = lax.axis_size("col")
    rows = lax.axis_size("row")
    both = ("row", "col")

    def diagonal(block, dr, dc):
        pairs = [
            ((r - dr) * cols + (c - dc), r * cols + c)
            for r in range(max(dr, 0), rows + min(dr, 0))
            for c in range(max(dc, 0), cols + min(dc, 0))
        ]
        return lax.ppermute(block, both, pairs)

    last_rows = cells[:, height - HALO :]
    first_rows = cells[:, :HALO]
    top = lax.ppermute(last_rows, "row", [(i, i + 1) for i in range(rows - 1)])
    bottom = lax.ppermute(first_rows, "row", [(i + 1, i) for i in range(rows - 1)])
    left = lax.ppermute(
        jnp.swapaxes(cells[:, :, breadth - HALO :], 1, 2), "col", [(i, i + 1) for i in range(cols - 1)]
    )
    right = lax.ppermute(jnp.swapaxes(cells[:, :, :HALO], 1, 2), "col", [(i + 1, i) for i in range(cols - 1)])
    top_left = diagonal(last_rows[:, :, breadth - HALO :], 1, 1)
    top_right = diagonal(last_rows[:, :, :HALO], 1, -1)
    bottom_left = diagonal(first_rows[:, :, breadth - HALO :], -1, 1)
    bottom_right = diagonal(first_rows[:, :, :HALO], -1, -1)

    def gap(count):
        return jnp.zeros((depth, count, LANE - 2 * HALO), cells.dtype)

    band = jnp.concatenate([cells, jnp.swapaxes(right, 1, 2), gap(height), jnp.swapaxes(left, 1, 2)], axis=2)
    upper = jnp.concatenate([top, top_right, gap(HALO), top_left], axis=2)
    lower = jnp.concatenate([bottom, bottom_right, gap(HALO), bottom_left], axis=2)
    pad = jnp.zeros((depth, SLACK, band.shape[2]), cells.dtype)
    return jnp.concatenate([pad, upper, band, lower, pad], axis=1)


def chunk_loop(count, body, unroll=1):
    lax.fori_loop(0, count, lambda c, carry: (body(c), carry)[1], 0, unroll=unroll)


def conductances(r_ref, cu, cd, cl, cr, dg, cv):
    layers, frame_rows, frame_cols = r_ref.shape
    count = (frame_rows - 2 * SLACK) // CHUNK

    def body(c):
        lead = pl.multiple_of(c * CHUNK, 8)
        rows = pl.ds(pl.multiple_of(lead + SLACK, 8), CHUNK)
        below = None
        for l in range(layers):
            win = r_ref[l, pl.ds(lead, CHUNK + 2 * SLACK), :]
            r = win[SLACK : SLACK + CHUNK]
            up = r * pltpu.roll(win, 1, 0)[SLACK : SLACK + CHUNK]
            down = r * pltpu.roll(win, CHUNK + 2 * SLACK - 1, 0)[SLACK : SLACK + CHUNK]
            left = r * pltpu.roll(r, 1, 1)
            right = r * pltpu.roll(r, frame_cols - 1, 1)
            total = up + down + left + right
            cu[l, rows, :] = RATE * up
            cd[l, rows, :] = RATE * down
            cl[l, rows, :] = RATE * left
            cr[l, rows, :] = RATE * right
            if l + 1 < layers:
                vertical = r_ref[l + 1, rows, :] * r
                cv[l, rows, :] = RATE * vertical
                total = total + vertical
            if below is not None:
                total = total + below
            if l == layers - 1:
                total = total + AMBIENT_LOSS
            dg[l, rows, :] = 1.0 - RATE * total
            below = vertical if l + 1 < layers else None

    chunk_loop(count, body)


def explicit_step(src, dst, cu, cd, cl, cr, dg, cv, s_ref):
    layers, frame_rows, frame_cols = dst.shape
    count = (frame_rows - 2 * SLACK) // CHUNK

    def body(c):
        lead = pl.multiple_of(c * CHUNK, 8)
        rows = pl.ds(pl.multiple_of(lead + SLACK, 8), CHUNK)
        above = pl.ds(pl.multiple_of(lead + SLACK - 8, 8), 8)
        below = pl.ds(pl.multiple_of(lead + SLACK + CHUNK, 8), 8)
        centre = [src[0, rows, :]] + [None] * (layers - 1)
        lower = None
        for l in range(layers):
            f = centre[l]
            win = jnp.concatenate([src[l, above, :], f, src[l, below, :]], axis=0)
            size = win.shape[0]
            up = pltpu.roll(win, 1, 0)[8 : 8 + CHUNK]
            down = pltpu.roll(win, size - 1, 0)[8 : 8 + CHUNK]
            left = pltpu.roll(f, 1, 1)
            right = pltpu.roll(f, frame_cols - 1, 1)
            value = dg[l, rows, :] * f + cu[l, rows, :] * up
            value = value + cd[l, rows, :] * down
            value = value + cl[l, rows, :] * left
            value = value + cr[l, rows, :] * right
            upper = None
            if l + 1 < layers:
                centre[l + 1] = src[l + 1, rows, :]
                upper = cv[l, rows, :]
                value = value + upper * centre[l + 1]
            if l > 0:
                value = value + lower * centre[l - 1]
            if l == 0 and s_ref is not None:
                value = value + RATE * s_ref[rows, :]
            dst[l, rows, :] = value
            lower = upper

    chunk_loop(count, body, 6)


def clear_slack(buf):
    layers, frame_rows, frame_cols = buf.shape
    zero = jnp.zeros((layers, SLACK, frame_cols), buf.dtype)
    buf[:, 0:SLACK, :] = zero
    buf[:, frame_rows - SLACK : frame_rows, :] = zero


def copy_center(src_view, dst_ref, height, breadth):
    def body(c):
        rows = pl.ds(pl.multiple_of(c * CHUNK, 8), CHUNK)
        from_rows = pl.ds(pl.multiple_of(c * CHUNK + SLACK + HALO, 8), CHUNK)
        dst_ref(rows, src_view(from_rows, breadth))

    chunk_loop(height // CHUNK, body)


def solve_kernel(f_ref, r_ref, s_ref, t_ref, out_ref, grad_ref, gsum_ref, cu, cd, cl, cr, dg, cv, a, b):
    layers, height, breadth = out_ref.shape
    frame_rows = a.shape[1]
    clear_slack(a)
    clear_slack(b)
    conductances(r_ref, cu, cd, cl, cr, dg, cv)
    src = f_ref
    for index in range(STEPS):
        dst = a if index % 2 == 0 else b
        explicit_step(src, dst, cu, cd, cl, cr, dg, cv, s_ref)
        src = dst

    def put(rows, value):
        out_ref[:, rows, :] = value

    copy_center(lambda rows, width, v=src: v[:, rows, 0:width], put, height, breadth)
    final = src
    start = b if final is a else a
    start[1:] = jnp.zeros((layers - 1,) + start.shape[1:], start.dtype)

    def seed(c):
        rows = pl.ds(pl.multiple_of(c * CHUNK, 8), CHUNK)
        start[0, rows, :] = final[0, rows, :] - t_ref[rows, :]

    chunk_loop(frame_rows // CHUNK, seed)
    src = start
    for index in range(STEPS):
        view = src

        def put_sum(rows, value, first=(index == 0)):
            if first:
                gsum_ref[rows, :] = value
            else:
                gsum_ref[rows, :] = gsum_ref[rows, :] + value

        copy_center(lambda rows, width, v=view: v[0, rows, 0:width], put_sum, height, breadth)
        dst = final if src is start else start
        explicit_step(src, dst, cu, cd, cl, cr, dg, cv, None)
        src = dst

    def put_grad(rows, value):
        grad_ref[:, rows, :] = value

    copy_center(lambda rows, width, v=src: v[:, rows, 0:width], put_grad, height, breadth)


def stencil_scratch(layers, frame_rows, frame_cols):
    whole = pltpu.VMEM((layers, frame_rows, frame_cols), jnp.float32)
    return [whole] * 5 + [pltpu.VMEM((layers - 1, frame_rows, frame_cols), jnp.float32), whole, whole]


def vmem_specs(count):
    return [pl.BlockSpec(memory_space=pltpu.VMEM) for _ in range(count)]


def run_solve(f_frame, r_frame, s_frame, t_frame, height, breadth):
    layers, frame_rows, frame_cols = f_frame.shape
    field = jax.ShapeDtypeStruct((layers, height, breadth), jnp.float32)
    return pl.pallas_call(
        solve_kernel,
        out_shape=(field, field, jax.ShapeDtypeStruct((height, breadth), jnp.float32)),
        in_specs=vmem_specs(4),
        out_specs=tuple(vmem_specs(3)),
        scratch_shapes=stencil_scratch(layers, frame_rows, frame_cols),
        compiler_params=pltpu.CompilerParams(vmem_limit_bytes=60 * 1024 * 1024),
    )(f_frame, r_frame, s_frame, t_frame)


def send_dies(outbound, row_count, col_count):
    received = lax.all_to_all(
        outbound.reshape(row_count * col_count, CAP, -1),
        ("row", "col"),
        split_axis=0,
        concat_axis=0,
        tiled=True,
    )
    return received.reshape(row_count * col_count * CAP, -1)


def return_grads(backward, row_count, col_count):
    returned = lax.all_to_all(
        backward.reshape(row_count * col_count, CAP, -1),
        ("row", "col"),
        split_axis=0,
        concat_axis=0,
        tiled=True,
    )
    return returned.reshape(row_count * col_count * CAP, -1)


def on_device(init_temp, power, die_owner, die_tile, classes, cond_table, target):
    row_count = lax.axis_size("row")
    col_count = lax.axis_size("col")
    devices_all = row_count * col_count
    layers, height, breadth = init_temp.shape
    tile_rows = height // TILE
    tile_cols = breadth // TILE
    die_count = power.shape[0]
    highest = lax.Precision.HIGHEST
    power_flat = power.reshape(die_count, TILE * TILE)
    owners = die_owner[:, 0]
    ordinal = jnp.arange(die_count, dtype=jnp.int32)
    same_owner = (owners[:, None] == owners[None, :]) & (ordinal[:, None] < ordinal[None, :])
    ranking = jnp.sum(same_owner.astype(jnp.int32), axis=0)
    slot_index = owners * CAP + ranking
    all_slots = jnp.arange(devices_all * CAP, dtype=jnp.int32)
    matched = all_slots[:, None] == slot_index[None, :]
    send_hot = matched.astype(jnp.float32)
    tile_column = jnp.zeros((die_count, LANE), jnp.float32).at[:, 0].set((die_tile + 1).astype(jnp.float32))
    outbound = jnp.dot(send_hot, jnp.concatenate([power_flat, tile_column], 1), precision=highest)
    received = send_dies(outbound, row_count, col_count)
    recv_tiles = received[:, TILE * TILE].astype(jnp.int32) - 1
    received = received[:, : TILE * TILE]
    tile_range = jnp.arange(tile_rows * tile_cols, dtype=jnp.int32)
    recv_hot = (tile_range[:, None] == recv_tiles[None, :]).astype(jnp.float32)
    source_tiles = jnp.dot(recv_hot, received, precision=highest)
    source = (
        source_tiles.reshape(tile_rows, tile_cols, TILE, TILE)
        .transpose(0, 2, 1, 3)
        .reshape(height, breadth)
    )
    root_cond = conduct_root(classes, cond_table)
    r_frame = framed(root_cond)
    s_frame = framed(source[None])[0]
    f_frame = framed(init_temp)
    t_frame = framed(target[None])[0]
    heat_field, adjoint, grad_sum = run_solve(f_frame, r_frame, s_frame, t_frame, height, breadth)
    grad_tiles = (
        grad_sum.reshape(tile_rows, TILE, tile_cols, TILE)
        .transpose(0, 2, 1, 3)
        .reshape(tile_rows * tile_cols, TILE * TILE)
    )
    backward = jnp.dot(recv_hot.T, grad_tiles, precision=highest)
    returned = return_grads(backward, row_count, col_count)
    die_grad = (RATE * jnp.dot(send_hot.T, returned, precision=highest)).reshape(
        die_count, TILE, TILE
    )
    return (heat_field, adjoint, die_grad)


def solution(mesh):
    in_specs = (
        P(None, "row", "col"),
        P(("row", "col"), None, None),
        P(("row", "col"), None),
        P(("row", "col")),
        P(None, "row", "col"),
        P(),
        P("row", "col"),
    )
    out_specs = (P(None, "row", "col"), P(None, "row", "col"), P(("row", "col"), None, None))
    return jax.shard_map(
        on_device, mesh=mesh, in_specs=in_specs, out_specs=out_specs, check_vma=False
    )
```

```python
import jax
import jax.numpy as jnp
from jax import lax
from jax.experimental import pallas as pl
from jax.experimental.pallas import tpu as pltpu
from jax.sharding import PartitionSpec as P

TILE = 64
CLASSES = 8
STEPS = 6
CAP = 2


RATE = 0.1
AMBIENT_LOSS = 0.3


def extended(cells, sides, width):
    for axis, dim in sides:
        count = lax.axis_size(axis)
        ends = count - 1
        head = lax.slice_in_dim(cells, 0, width, axis=dim)
        tail = lax.slice_in_dim(cells, cells.shape[dim] - width, cells.shape[dim], axis=dim)
        cells = jnp.concatenate(
            [
                lax.ppermute(tail, axis, [(i, (i + 1) % count) for i in range(ends)]),
                cells,
                lax.ppermute(head, axis, [((i + 1) % count, i) for i in range(ends)]),
            ],
            axis=dim,
        )
    return cells


def conduct_root(classes, cond_table):
    conduct = jnp.zeros(classes.shape, cond_table.dtype)
    for label in range(CLASSES):
        conduct = conduct + jnp.where(classes == label, cond_table[:, label][:, None, None], 0.0)
    return jnp.sqrt(conduct)


def advance(field, root_cond, source):
    middle = field[:, 1:-1, 1:-1]
    roots = root_cond[:, 1:-1, 1:-1]
    inflow = roots * root_cond[:, :-2, 1:-1] * (field[:, :-2, 1:-1] - middle)
    inflow = inflow + roots * root_cond[:, 2:, 1:-1] * (field[:, 2:, 1:-1] - middle)
    inflow = inflow + roots * root_cond[:, 1:-1, :-2] * (field[:, 1:-1, :-2] - middle)
    inflow = inflow + roots * root_cond[:, 1:-1, 2:] * (field[:, 1:-1, 2:] - middle)
    vertical = roots[1:] * roots[:-1] * (middle[1:] - middle[:-1])
    zero_layer = jnp.zeros_like(middle[:1])
    inflow = (
        inflow
        + jnp.concatenate([vertical, zero_layer], 0)
        - jnp.concatenate([zero_layer, vertical], 0)
    )
    inflow = inflow - AMBIENT_LOSS * jnp.concatenate([jnp.zeros_like(middle[:-1]), middle[-1:]], 0)
    if source is not None:
        inflow = inflow + jnp.concatenate([source[None], jnp.zeros_like(middle[1:])], 0)
    return middle + RATE * inflow


HALO = 16
SLACK = 8
CHUNK = 8
LANE = 128


def framed(cells):
    depth, height, breadth = cells.shape
    cols = lax.axis_size("col")
    rows = lax.axis_size("row")
    left = lax.ppermute(
        jnp.swapaxes(cells[:, :, breadth - HALO :], 1, 2), "col", [(i, i + 1) for i in range(cols - 1)]
    )
    right = lax.ppermute(jnp.swapaxes(cells[:, :, :HALO], 1, 2), "col", [(i + 1, i) for i in range(cols - 1)])
    left = jnp.swapaxes(left, 1, 2)
    right = jnp.swapaxes(right, 1, 2)
    gap = jnp.zeros((depth, height, LANE - 2 * HALO), cells.dtype)
    band = jnp.concatenate([cells, right, gap, left], axis=2)
    top = lax.ppermute(band[:, height - HALO :], "row", [(i, i + 1) for i in range(rows - 1)])
    bottom = lax.ppermute(band[:, :HALO], "row", [(i + 1, i) for i in range(rows - 1)])
    pad = jnp.zeros((depth, SLACK, band.shape[2]), cells.dtype)
    return jnp.concatenate([pad, top, band, bottom, pad], axis=1)


def chunk_loop(count, body):
    lax.fori_loop(0, count, lambda c, carry: (body(c), carry)[1], 0, unroll=9)


def conductances(r_ref, cu, cd, cl, cr, dg, cv):
    layers, frame_rows, frame_cols = r_ref.shape
    count = (frame_rows - 2 * SLACK) // CHUNK

    def body(c):
        lead = pl.multiple_of(c * CHUNK, 8)
        rows = pl.ds(pl.multiple_of(lead + SLACK, 8), CHUNK)
        below = None
        for l in range(layers):
            win = r_ref[l, pl.ds(lead, CHUNK + 2 * SLACK), :]
            r = win[SLACK : SLACK + CHUNK]
            up = r * pltpu.roll(win, 1, 0)[SLACK : SLACK + CHUNK]
            down = r * pltpu.roll(win, CHUNK + 2 * SLACK - 1, 0)[SLACK : SLACK + CHUNK]
            left = r * pltpu.roll(r, 1, 1)
            right = r * pltpu.roll(r, frame_cols - 1, 1)
            total = up + down + left + right
            cu[l, rows, :] = RATE * up
            cd[l, rows, :] = RATE * down
            cl[l, rows, :] = RATE * left
            cr[l, rows, :] = RATE * right
            if l + 1 < layers:
                vertical = r_ref[l + 1, rows, :] * r
                cv[l, rows, :] = RATE * vertical
                total = total + vertical
            if below is not None:
                total = total + below
            if l == layers - 1:
                total = total + AMBIENT_LOSS
            dg[l, rows, :] = 1.0 - RATE * total
            below = vertical if l + 1 < layers else None

    chunk_loop(count, body)


def explicit_step(src, dst, cu, cd, cl, cr, dg, cv, s_ref):
    layers, frame_rows, frame_cols = dst.shape
    count = (frame_rows - 2 * SLACK) // CHUNK

    def body(c):
        lead = pl.multiple_of(c * CHUNK, 8)
        rows = pl.ds(pl.multiple_of(lead + SLACK, 8), CHUNK)
        above = pl.ds(pl.multiple_of(lead + SLACK - 8, 8), 8)
        below = pl.ds(pl.multiple_of(lead + SLACK + CHUNK, 8), 8)
        centre = [src[0, rows, :]] + [None] * (layers - 1)
        lower = None
        for l in range(layers):
            f = centre[l]
            win = jnp.concatenate([src[l, above, :], f, src[l, below, :]], axis=0)
            size = win.shape[0]
            up = pltpu.roll(win, 1, 0)[8 : 8 + CHUNK]
            down = pltpu.roll(win, size - 1, 0)[8 : 8 + CHUNK]
            left = pltpu.roll(f, 1, 1)
            right = pltpu.roll(f, frame_cols - 1, 1)
            value = dg[l, rows, :] * f + cu[l, rows, :] * up
            value = value + cd[l, rows, :] * down
            value = value + cl[l, rows, :] * left
            value = value + cr[l, rows, :] * right
            upper = None
            if l + 1 < layers:
                centre[l + 1] = src[l + 1, rows, :]
                upper = cv[l, rows, :]
                value = value + upper * centre[l + 1]
            if l > 0:
                value = value + lower * centre[l - 1]
            if l == 0 and s_ref is not None:
                value = value + RATE * s_ref[rows, :]
            dst[l, rows, :] = value
            lower = upper

    chunk_loop(count, body)


def clear_slack(buf):
    layers, frame_rows, frame_cols = buf.shape
    zero = jnp.zeros((layers, SLACK, frame_cols), buf.dtype)
    buf[:, 0:SLACK, :] = zero
    buf[:, frame_rows - SLACK : frame_rows, :] = zero


def copy_center(src_view, dst_ref, height, breadth):
    def body(c):
        rows = pl.ds(pl.multiple_of(c * CHUNK, 8), CHUNK)
        from_rows = pl.ds(pl.multiple_of(c * CHUNK + SLACK + HALO, 8), CHUNK)
        dst_ref(rows, src_view(from_rows, breadth))

    chunk_loop(height // CHUNK, body)


def solve_kernel(f_ref, r_ref, s_ref, t_ref, out_ref, grad_ref, gsum_ref, cu, cd, cl, cr, dg, cv, a, b):
    layers, height, breadth = out_ref.shape
    frame_rows = a.shape[1]
    clear_slack(a)
    clear_slack(b)
    conductances(r_ref, cu, cd, cl, cr, dg, cv)
    src = f_ref
    for index in range(STEPS):
        dst = a if index % 2 == 0 else b
        explicit_step(src, dst, cu, cd, cl, cr, dg, cv, s_ref)
        src = dst

    def put(rows, value):
        out_ref[:, rows, :] = value

    copy_center(lambda rows, width, v=src: v[:, rows, 0:width], put, height, breadth)
    final = src
    start = b if final is a else a
    start[1:] = jnp.zeros((layers - 1,) + start.shape[1:], start.dtype)

    def seed(c):
        rows = pl.ds(pl.multiple_of(c * CHUNK, 8), CHUNK)
        start[0, rows, :] = final[0, rows, :] - t_ref[rows, :]

    chunk_loop(frame_rows // CHUNK, seed)
    src = start
    for index in range(STEPS):
        view = src

        def put_sum(rows, value, first=(index == 0)):
            if first:
                gsum_ref[rows, :] = value
            else:
                gsum_ref[rows, :] = gsum_ref[rows, :] + value

        copy_center(lambda rows, width, v=view: v[0, rows, 0:width], put_sum, height, breadth)
        dst = final if src is start else start
        explicit_step(src, dst, cu, cd, cl, cr, dg, cv, None)
        src = dst

    def put_grad(rows, value):
        grad_ref[:, rows, :] = value

    copy_center(lambda rows, width, v=src: v[:, rows, 0:width], put_grad, height, breadth)


def stencil_scratch(layers, frame_rows, frame_cols):
    whole = pltpu.VMEM((layers, frame_rows, frame_cols), jnp.float32)
    return [whole] * 5 + [pltpu.VMEM((layers - 1, frame_rows, frame_cols), jnp.float32), whole, whole]


def vmem_specs(count):
    return [pl.BlockSpec(memory_space=pltpu.VMEM) for _ in range(count)]


def run_solve(f_frame, r_frame, s_frame, t_frame, height, breadth):
    layers, frame_rows, frame_cols = f_frame.shape
    field = jax.ShapeDtypeStruct((layers, height, breadth), jnp.float32)
    return pl.pallas_call(
        solve_kernel,
        out_shape=(field, field, jax.ShapeDtypeStruct((height, breadth), jnp.float32)),
        in_specs=vmem_specs(4),
        out_specs=tuple(vmem_specs(3)),
        scratch_shapes=stencil_scratch(layers, frame_rows, frame_cols),
        compiler_params=pltpu.CompilerParams(vmem_limit_bytes=60 * 1024 * 1024),
    )(f_frame, r_frame, s_frame, t_frame)


def on_device(init_temp, power, die_owner, die_tile, classes, cond_table, target):
    row_count = lax.axis_size("row")
    col_count = lax.axis_size("col")
    devices_all = row_count * col_count
    layers, height, breadth = init_temp.shape
    tile_rows = height // TILE
    tile_cols = breadth // TILE
    die_count = power.shape[0]
    highest = lax.Precision.HIGHEST
    power_flat = power.reshape(die_count, TILE * TILE)
    owners = die_owner[:, 0]
    ordinal = jnp.arange(die_count, dtype=jnp.int32)
    same_owner = (owners[:, None] == owners[None, :]) & (ordinal[:, None] < ordinal[None, :])
    ranking = jnp.sum(same_owner.astype(jnp.int32), axis=0)
    slot_index = owners * CAP + ranking
    all_slots = jnp.arange(devices_all * CAP, dtype=jnp.int32)
    matched = all_slots[:, None] == slot_index[None, :]
    send_hot = matched.astype(jnp.float32).reshape(devices_all, CAP, die_count)
    tile_column = jnp.zeros((die_count, LANE), jnp.float32).at[:, 0].set((die_tile + 1).astype(jnp.float32))
    payload = jnp.concatenate([power_flat, tile_column], 1)
    outbound = jnp.einsum("dck,kn->dcn", send_hot, payload, precision=highest)
    received = lax.all_to_all(outbound, ("row", "col"), split_axis=0, concat_axis=0, tiled=True)
    recv_tiles = received[:, :, TILE * TILE].astype(jnp.int32) - 1
    tile_range = jnp.arange(tile_rows * tile_cols, dtype=jnp.int32)
    recv_hot = (tile_range[:, None, None] == recv_tiles[None]).astype(jnp.float32)
    source_tiles = jnp.einsum("tdc,dcn->tn", recv_hot, received[:, :, : TILE * TILE], precision=highest)
    source = (
        source_tiles.reshape(tile_rows, tile_cols, TILE, TILE)
        .transpose(0, 2, 1, 3)
        .reshape(height, breadth)
    )
    root_cond = conduct_root(classes, cond_table)
    r_frame = framed(root_cond)
    s_frame = framed(source[None])[0]
    f_frame = framed(init_temp)
    t_frame = framed(target[None])[0]
    heat_field, adjoint, grad_sum = run_solve(f_frame, r_frame, s_frame, t_frame, height, breadth)
    grad_tiles = (
        grad_sum.reshape(tile_rows, TILE, tile_cols, TILE)
        .transpose(0, 2, 1, 3)
        .reshape(tile_rows * tile_cols, TILE * TILE)
    )
    backward = jnp.einsum("tdc,tn->dcn", recv_hot, grad_tiles, precision=highest)
    returned = lax.all_to_all(backward, ("row", "col"), split_axis=0, concat_axis=0, tiled=True)
    die_grad = (RATE * jnp.einsum("dck,dcn->kn", send_hot, returned, precision=highest)).reshape(
        die_count, TILE, TILE
    )
    return (heat_field, adjoint, die_grad)


def solution(mesh):
    in_specs = (
        P(None, "row", "col"),
        P(("row", "col"), None, None),
        P(("row", "col"), None),
        P(("row", "col")),
        P(None, "row", "col"),
        P(),
        P("row", "col"),
    )
    out_specs = (P(None, "row", "col"), P(None, "row", "col"), P(("row", "col"), None, None))
    return jax.shard_map(
        on_device, mesh=mesh, in_specs=in_specs, out_specs=out_specs, check_vma=False
    )
```

```python
import jax
import jax.numpy as jnp
from jax import lax
from jax.experimental import pallas as pl
from jax.experimental.pallas import tpu as pltpu
from jax.sharding import PartitionSpec as P

TILE = 64
CLASSES = 8
STEPS = 6
CAP = 2


RATE = 0.1
AMBIENT_LOSS = 0.3


def extended(cells, sides, width):
    for axis, dim in sides:
        count = lax.axis_size(axis)
        ends = count - 1
        head = lax.slice_in_dim(cells, 0, width, axis=dim)
        tail = lax.slice_in_dim(cells, cells.shape[dim] - width, cells.shape[dim], axis=dim)
        cells = jnp.concatenate(
            [
                lax.ppermute(tail, axis, [(i, (i + 1) % count) for i in range(ends)]),
                cells,
                lax.ppermute(head, axis, [((i + 1) % count, i) for i in range(ends)]),
            ],
            axis=dim,
        )
    return cells


def conduct_root(classes, cond_table):
    conduct = jnp.zeros(classes.shape, cond_table.dtype)
    for label in range(CLASSES):
        conduct = conduct + jnp.where(classes == label, cond_table[:, label][:, None, None], 0.0)
    return jnp.sqrt(conduct)


def advance(field, root_cond, source):
    middle = field[:, 1:-1, 1:-1]
    roots = root_cond[:, 1:-1, 1:-1]
    inflow = roots * root_cond[:, :-2, 1:-1] * (field[:, :-2, 1:-1] - middle)
    inflow = inflow + roots * root_cond[:, 2:, 1:-1] * (field[:, 2:, 1:-1] - middle)
    inflow = inflow + roots * root_cond[:, 1:-1, :-2] * (field[:, 1:-1, :-2] - middle)
    inflow = inflow + roots * root_cond[:, 1:-1, 2:] * (field[:, 1:-1, 2:] - middle)
    vertical = roots[1:] * roots[:-1] * (middle[1:] - middle[:-1])
    zero_layer = jnp.zeros_like(middle[:1])
    inflow = (
        inflow
        + jnp.concatenate([vertical, zero_layer], 0)
        - jnp.concatenate([zero_layer, vertical], 0)
    )
    inflow = inflow - AMBIENT_LOSS * jnp.concatenate([jnp.zeros_like(middle[:-1]), middle[-1:]], 0)
    if source is not None:
        inflow = inflow + jnp.concatenate([source[None], jnp.zeros_like(middle[1:])], 0)
    return middle + RATE * inflow


HALO = 16
SLACK = 8
CHUNK = 8
LANE = 128


def framed(cells):
    depth, height, breadth = cells.shape
    cols = lax.axis_size("col")
    rows = lax.axis_size("row")
    left = lax.ppermute(
        jnp.swapaxes(cells[:, :, breadth - HALO :], 1, 2), "col", [(i, i + 1) for i in range(cols - 1)]
    )
    right = lax.ppermute(jnp.swapaxes(cells[:, :, :HALO], 1, 2), "col", [(i + 1, i) for i in range(cols - 1)])
    left = jnp.swapaxes(left, 1, 2)
    right = jnp.swapaxes(right, 1, 2)
    gap = jnp.zeros((depth, height, LANE - 2 * HALO), cells.dtype)
    band = jnp.concatenate([cells, right, gap, left], axis=2)
    top = lax.ppermute(band[:, height - HALO :], "row", [(i, i + 1) for i in range(rows - 1)])
    bottom = lax.ppermute(band[:, :HALO], "row", [(i + 1, i) for i in range(rows - 1)])
    pad = jnp.zeros((depth, SLACK, band.shape[2]), cells.dtype)
    return jnp.concatenate([pad, top, band, bottom, pad], axis=1)


def chunk_loop(count, body):
    lax.fori_loop(0, count, lambda c, carry: (body(c), carry)[1], 0, unroll=9)


def conductances(r_ref, cu, cd, cl, cr, dg, cv):
    layers, frame_rows, frame_cols = r_ref.shape
    count = (frame_rows - 2 * SLACK) // CHUNK

    def body(c):
        lead = pl.multiple_of(c * CHUNK, 8)
        rows = pl.ds(pl.multiple_of(lead + SLACK, 8), CHUNK)
        below = None
        for l in range(layers):
            win = r_ref[l, pl.ds(lead, CHUNK + 2 * SLACK), :]
            r = win[SLACK : SLACK + CHUNK]
            up = r * pltpu.roll(win, 1, 0)[SLACK : SLACK + CHUNK]
            down = r * pltpu.roll(win, CHUNK + 2 * SLACK - 1, 0)[SLACK : SLACK + CHUNK]
            left = r * pltpu.roll(r, 1, 1)
            right = r * pltpu.roll(r, frame_cols - 1, 1)
            total = up + down + left + right
            cu[l, rows, :] = RATE * up
            cd[l, rows, :] = RATE * down
            cl[l, rows, :] = RATE * left
            cr[l, rows, :] = RATE * right
            if l + 1 < layers:
                vertical = r_ref[l + 1, rows, :] * r
                cv[l, rows, :] = RATE * vertical
                total = total + vertical
            if below is not None:
                total = total + below
            if l == layers - 1:
                total = total + AMBIENT_LOSS
            dg[l, rows, :] = 1.0 - RATE * total
            below = vertical if l + 1 < layers else None

    chunk_loop(count, body)


def explicit_step(src, dst, cu, cd, cl, cr, dg, cv, s_ref):
    layers, frame_rows, frame_cols = dst.shape
    count = (frame_rows - 2 * SLACK) // CHUNK

    def body(c):
        lead = pl.multiple_of(c * CHUNK, 8)
        rows = pl.ds(pl.multiple_of(lead + SLACK, 8), CHUNK)
        above = pl.ds(pl.multiple_of(lead + SLACK - 8, 8), 8)
        below = pl.ds(pl.multiple_of(lead + SLACK + CHUNK, 8), 8)
        centre = [src[0, rows, :]] + [None] * (layers - 1)
        lower = None
        for l in range(layers):
            f = centre[l]
            win = jnp.concatenate([src[l, above, :], f, src[l, below, :]], axis=0)
            size = win.shape[0]
            up = pltpu.roll(win, 1, 0)[8 : 8 + CHUNK]
            down = pltpu.roll(win, size - 1, 0)[8 : 8 + CHUNK]
            left = pltpu.roll(f, 1, 1)
            right = pltpu.roll(f, frame_cols - 1, 1)
            value = dg[l, rows, :] * f + cu[l, rows, :] * up
            value = value + cd[l, rows, :] * down
            value = value + cl[l, rows, :] * left
            value = value + cr[l, rows, :] * right
            upper = None
            if l + 1 < layers:
                centre[l + 1] = src[l + 1, rows, :]
                upper = cv[l, rows, :]
                value = value + upper * centre[l + 1]
            if l > 0:
                value = value + lower * centre[l - 1]
            if l == 0 and s_ref is not None:
                value = value + RATE * s_ref[rows, :]
            dst[l, rows, :] = value
            lower = upper

    chunk_loop(count, body)


def clear_slack(buf):
    layers, frame_rows, frame_cols = buf.shape
    zero = jnp.zeros((layers, SLACK, frame_cols), buf.dtype)
    buf[:, 0:SLACK, :] = zero
    buf[:, frame_rows - SLACK : frame_rows, :] = zero


def copy_center(src_view, dst_ref, height, breadth):
    def body(c):
        rows = pl.ds(pl.multiple_of(c * CHUNK, 8), CHUNK)
        from_rows = pl.ds(pl.multiple_of(c * CHUNK + SLACK + HALO, 8), CHUNK)
        dst_ref(rows, src_view(from_rows, breadth))

    chunk_loop(height // CHUNK, body)


def solve_kernel(f_ref, r_ref, s_ref, t_ref, out_ref, grad_ref, gsum_ref, cu, cd, cl, cr, dg, cv, a, b):
    layers, height, breadth = out_ref.shape
    frame_rows = a.shape[1]
    clear_slack(a)
    clear_slack(b)
    conductances(r_ref, cu, cd, cl, cr, dg, cv)
    src = f_ref
    for index in range(STEPS):
        dst = a if index % 2 == 0 else b
        explicit_step(src, dst, cu, cd, cl, cr, dg, cv, s_ref)
        src = dst

    def put(rows, value):
        out_ref[:, rows, :] = value

    copy_center(lambda rows, width, v=src: v[:, rows, 0:width], put, height, breadth)
    final = src
    start = b if final is a else a
    start[1:] = jnp.zeros((layers - 1,) + start.shape[1:], start.dtype)

    def seed(c):
        rows = pl.ds(pl.multiple_of(c * CHUNK, 8), CHUNK)
        start[0, rows, :] = final[0, rows, :] - t_ref[rows, :]

    chunk_loop(frame_rows // CHUNK, seed)
    src = start
    for index in range(STEPS):
        view = src

        def put_sum(rows, value, first=(index == 0)):
            if first:
                gsum_ref[rows, :] = value
            else:
                gsum_ref[rows, :] = gsum_ref[rows, :] + value

        copy_center(lambda rows, width, v=view: v[0, rows, 0:width], put_sum, height, breadth)
        dst = final if src is start else start
        explicit_step(src, dst, cu, cd, cl, cr, dg, cv, None)
        src = dst

    def put_grad(rows, value):
        grad_ref[:, rows, :] = value

    copy_center(lambda rows, width, v=src: v[:, rows, 0:width], put_grad, height, breadth)


def stencil_scratch(layers, frame_rows, frame_cols):
    whole = pltpu.VMEM((layers, frame_rows, frame_cols), jnp.float32)
    return [whole] * 5 + [pltpu.VMEM((layers - 1, frame_rows, frame_cols), jnp.float32), whole, whole]


def vmem_specs(count):
    return [pl.BlockSpec(memory_space=pltpu.VMEM) for _ in range(count)]


def run_solve(f_frame, r_frame, s_frame, t_frame, height, breadth):
    layers, frame_rows, frame_cols = f_frame.shape
    field = jax.ShapeDtypeStruct((layers, height, breadth), jnp.float32)
    return pl.pallas_call(
        solve_kernel,
        out_shape=(field, field, jax.ShapeDtypeStruct((height, breadth), jnp.float32)),
        in_specs=vmem_specs(4),
        out_specs=tuple(vmem_specs(3)),
        scratch_shapes=stencil_scratch(layers, frame_rows, frame_cols),
        compiler_params=pltpu.CompilerParams(vmem_limit_bytes=60 * 1024 * 1024),
    )(f_frame, r_frame, s_frame, t_frame)


def send_dies(outbound, row_count, col_count):
    received = lax.all_to_all(
        outbound.reshape(row_count * col_count, CAP, -1),
        ("row", "col"),
        split_axis=0,
        concat_axis=0,
        tiled=True,
    )
    return received.reshape(row_count * col_count * CAP, -1)


def return_grads(backward, row_count, col_count):
    returned = lax.all_to_all(
        backward.reshape(row_count * col_count, CAP, -1),
        ("row", "col"),
        split_axis=0,
        concat_axis=0,
        tiled=True,
    )
    return returned.reshape(row_count * col_count * CAP, -1)


def on_device(init_temp, power, die_owner, die_tile, classes, cond_table, target):
    row_count = lax.axis_size("row")
    col_count = lax.axis_size("col")
    devices_all = row_count * col_count
    layers, height, breadth = init_temp.shape
    tile_rows = height // TILE
    tile_cols = breadth // TILE
    die_count = power.shape[0]
    highest = lax.Precision.HIGHEST
    power_flat = power.reshape(die_count, TILE * TILE)
    owners = die_owner[:, 0]
    ordinal = jnp.arange(die_count, dtype=jnp.int32)
    same_owner = (owners[:, None] == owners[None, :]) & (ordinal[:, None] < ordinal[None, :])
    ranking = jnp.sum(same_owner.astype(jnp.int32), axis=0)
    slot_index = owners * CAP + ranking
    all_slots = jnp.arange(devices_all * CAP, dtype=jnp.int32)
    matched = all_slots[:, None] == slot_index[None, :]
    send_hot = matched.astype(jnp.float32)
    tile_column = jnp.zeros((die_count, LANE), jnp.float32).at[:, 0].set((die_tile + 1).astype(jnp.float32))
    outbound = jnp.dot(send_hot, jnp.concatenate([power_flat, tile_column], 1), precision=highest)
    received = send_dies(outbound, row_count, col_count)
    recv_tiles = received[:, TILE * TILE].astype(jnp.int32) - 1
    received = received[:, : TILE * TILE]
    tile_range = jnp.arange(tile_rows * tile_cols, dtype=jnp.int32)
    recv_hot = (tile_range[:, None] == recv_tiles[None, :]).astype(jnp.float32)
    source_tiles = jnp.dot(recv_hot, received, precision=highest)
    source = (
        source_tiles.reshape(tile_rows, tile_cols, TILE, TILE)
        .transpose(0, 2, 1, 3)
        .reshape(height, breadth)
    )
    root_cond = conduct_root(classes, cond_table)
    r_frame = framed(root_cond)
    s_frame = framed(source[None])[0]
    f_frame = framed(init_temp)
    t_frame = framed(target[None])[0]
    heat_field, adjoint, grad_sum = run_solve(f_frame, r_frame, s_frame, t_frame, height, breadth)
    grad_tiles = (
        grad_sum.reshape(tile_rows, TILE, tile_cols, TILE)
        .transpose(0, 2, 1, 3)
        .reshape(tile_rows * tile_cols, TILE * TILE)
    )
    recv_hot = recv_hot.reshape(tile_rows * tile_cols, row_count * col_count, CAP)
    backward = jnp.einsum("tdc,tn->dcn", recv_hot, grad_tiles, precision=highest)
    returned = lax.all_to_all(backward, ("row", "col"), split_axis=0, concat_axis=0, tiled=True)
    send_hot = send_hot.reshape(row_count * col_count, CAP, die_count)
    die_grad = (RATE * jnp.einsum("dck,dcn->kn", send_hot, returned, precision=highest)).reshape(
        die_count, TILE, TILE
    )
    return (heat_field, adjoint, die_grad)


def solution(mesh):
    in_specs = (
        P(None, "row", "col"),
        P(("row", "col"), None, None),
        P(("row", "col"), None),
        P(("row", "col")),
        P(None, "row", "col"),
        P(),
        P("row", "col"),
    )
    out_specs = (P(None, "row", "col"), P(None, "row", "col"), P(("row", "col"), None, None))
    return jax.shard_map(
        on_device, mesh=mesh, in_specs=in_specs, out_specs=out_specs, check_vma=False
    )
```
